256 devices in a mesh: gx: 8 (over y, core), gy: 32 (over z, x).
Axes of the slice: x: 4, y: 4, z: 8, core: 2. Of those that a mesh axis runs over, the one named last changes fastest.
Arguments:
- displacement: float32 [3, 64, 256, 128], P(None, 'gx', 'gy'), may hold values from -0.12 to 0.12
- velocity: float32 [3, 64, 256, 128], P(None, 'gx', 'gy'), may hold values from -4 to 4
- intact: int32 [61, 64, 256, 128], P(None, 'gx', 'gy'), may hold values 0 or 1
- material: int32 [64, 256, 128], P('gx', 'gy'), may hold values from 0 to 7
- bulk_modulus: float32 [8], replicated, may hold values from 80 to 800
- shear_modulus: float32 [8], replicated, may hold values from 40 to 400
- density: float32 [8], replicated, may hold values from 1 to 4
Outputs:
- new_displacement: float32 [3, 64, 256, 128], P(None, 'gx', 'gy')
- new_velocity: float32 [3, 64, 256, 128], P(None, 'gx', 'gy')
- last_force: float32 [3, 64, 256, 128], P(None, 'gx', 'gy')
The draws below stay inside these ranges and needn't reach their ends.
Inputs may be any that keep to these rules, and one draw needn't show every extreme that they name: intact[k, i] refers to the bond from node i to node i + e_k.
All inputs are finite; a program needn't handle non-finite values. No bound on the sum of `intact` on one device may be relied on, other than what follows from the above.
Results may differ from the reference program's by a relative error of at most 0.00002.
Values sent between devices are 32-bit elements; how exact they have to be, the bound alone decides.
No kernel may reach another device: no remote copies, remote signals or barrier semaphores. Data moves between devices by JAX's collectives and lax.ppermute only.
A program may use at most 64 MiB of HBM per device.

```python
import math
import jax
import jax.numpy as jnp

NZ = 128
STEPS = 2
BONDS = 61
CLASSES = 8
NX = 64
NY = 256


def set_ends(values, own_key, smallest, largest):
    index_at = [jax.random.randint(jax.random.fold_in(own_key, axis), (), 0, length) for axis, length in enumerate(values.shape)]
    main_axis = values.shape.index(max(values.shape))
    next_to = index_at[:main_axis] + [(index_at[main_axis] + 1) % values.shape[main_axis]] + index_at[main_axis + 1:]
    return values.at[tuple(index_at)].set(smallest).at[tuple(next_to)].set(largest)


def block_scale(stream_key, shape, shards, least, largest):
    level = 1.0
    for dim, blocks in shards:
        steps = jax.random.uniform(jax.random.fold_in(jax.random.fold_in(stream_key, 6), dim), (blocks,), jnp.float32, least / len(shards), largest / len(shards))
        level = level * jnp.repeat(jnp.exp(steps), shape[dim] // blocks).reshape((-1,) + (1,) * (len(shape) - 1 - dim))
    return level


def centred(key, dims, deviation, limit, pieces=(), kind=jnp.bfloat16):
    entries = jax.random.normal(key, dims, jnp.float32) * deviation
    if len(pieces) > 0:
        entries = block_scale(key, dims, pieces, -0.22, 0.18) * entries
    return jnp.clip(entries, min=-limit, max=limit).astype(kind)


def setup_inputs(seed: int = 0) -> dict:
    keys = jax.random.split(jax.random.key(seed), 8)
    displacement = centred(keys[0], (3, NX, NY, NZ), 0.03, 0.12, ((1, 8), (2, 32)), jnp.float32)
    velocity = centred(keys[1], (3, NX, NY, NZ), 1.0, 4.0, ((1, 8), (2, 32)), jnp.float32)
    intact = set_ends((jax.random.randint(keys[2], (BONDS, NX, NY, NZ), 0, 8) < 7).astype(jnp.int32), jax.random.fold_in(keys[2], 1), 0, 1)
    material = set_ends(jax.random.randint(keys[3], (NX, NY, NZ), 0, CLASSES), jax.random.fold_in(keys[3], 1), 0, CLASSES - 1).astype(jnp.int32)
    bulk_modulus = jnp.clip(jnp.exp(jax.random.uniform(keys[4], (CLASSES,), jnp.float32, math.log(80.0), math.log(800.0))), 80.0, 800.0)
    shear_modulus = jnp.clip(jnp.exp(jax.random.uniform(keys[5], (CLASSES,), jnp.float32, math.log(40.0), math.log(400.0))), 40.0, 400.0)
    density = jnp.clip(jnp.exp(jax.random.uniform(keys[6], (CLASSES,), jnp.float32, math.log(1.0), math.log(4.0))), 1.0, 4.0)
    return dict(displacement=displacement, velocity=velocity, intact=intact, material=material, bulk_modulus=bulk_modulus, shear_modulus=shear_modulus, density=density)


time_step = 0.02

def half_offsets():
    result = []
    for along_x in range(-3, 4):
        for along_y in range(-3, 4):
            for along_z in range(-3, 4):
                if along_x * along_x + along_y * along_y + along_z * along_z <= 9 and (along_x, along_y, along_z) > (0, 0, 0):
                    result.append((along_x, along_y, along_z))
    return result

def weighted_volume(offsets):
    return 2.0 * sum((math.sqrt(float(offset[0] * offset[0] + offset[1] * offset[1] + offset[2] * offset[2])) for offset in offsets))

def neighbour(padded, offset, extent):
    return padded[..., 3 + offset[0]:3 + offset[0] + extent[0], 3 + offset[1]:3 + offset[1] + extent[1], 3 + offset[2]:3 + offset[2] + extent[2]]

def stretch_terms(motion, padded_motion, offset, extent):
    partner = neighbour(padded_motion, offset, extent)
    radius = math.sqrt(float(offset[0] * offset[0] + offset[1] * offset[1] + offset[2] * offset[2]))
    components = [offset[number] + partner[number] - motion[number] for number in range(3)]
    length = jnp.sqrt(components[0] * components[0] + components[1] * components[1] + components[2] * components[2])
    return (components, length, length - radius, radius)

def node_force(motion, bulk_node, shear_node, intact, inside, offsets, volume):
    extent = bulk_node.shape
    padded_motion = jnp.pad(motion, ((0, 0), (3, 3), (3, 3), (3, 3)))
    own_sum = jnp.zeros(extent, jnp.float32)
    gathered = jnp.zeros(inside.shape, jnp.float32)
    for bond_index, offset in enumerate(offsets):
        components, length, stretch, radius = stretch_terms(motion, padded_motion, offset, extent)
        weight = intact[bond_index].astype(jnp.float32) * neighbour(inside, offset, extent)
        contribution = weight * stretch
        own_sum = own_sum + contribution
        gathered = gathered.at[3 + offset[0]:3 + offset[0] + extent[0], 3 + offset[1]:3 + offset[1] + extent[1], 3 + offset[2]:3 + offset[2] + extent[2]].add(contribution)
    dilatation = 3.0 / volume * (own_sum + gathered[3:-3, 3:-3, 3:-3])
    pressure = jnp.pad(bulk_node * dilatation, 3)
    shear_padded = jnp.pad(shear_node, 3)
    twisting = jnp.pad(shear_node * dilatation, 3)
    own_force = jnp.zeros(motion.shape, jnp.float32)
    returned = jnp.zeros(padded_motion.shape, jnp.float32)
    for bond_index, offset in enumerate(offsets):
        components, length, stretch, radius = stretch_terms(motion, padded_motion, offset, extent)
        weight = intact[bond_index].astype(jnp.float32) * neighbour(inside, offset, extent)
        tension = weight / radius * (3.0 * radius / volume * (bulk_node * dilatation + neighbour(pressure, offset, extent)) + 15.0 / volume * ((shear_node + neighbour(shear_padded, offset, extent)) * stretch - radius / 3.0 * (shear_node * dilatation + neighbour(twisting, offset, extent))))
        vector = jnp.stack([tension * component / length for component in components])
        own_force = own_force + vector
        returned = returned.at[:, 3 + offset[0]:3 + offset[0] + extent[0], 3 + offset[1]:3 + offset[1] + extent[1], 3 + offset[2]:3 + offset[2] + extent[2]].add(vector)
    return own_force - returned[:, 3:-3, 3:-3, 3:-3]

def reference(displacement, velocity, intact, material, bulk_modulus, shear_modulus, density):
    offsets = half_offsets()
    volume = weighted_volume(offsets)
    bulk_node = bulk_modulus[material]
    shear_node = shear_modulus[material]
    inertia = density[material]
    inside = jnp.pad(jnp.ones(material.shape, jnp.float32), 3)
    forces = jnp.zeros(displacement.shape, jnp.float32)
    for counter in range(STEPS):
        forces = node_force(displacement, bulk_node, shear_node, intact, inside, offsets, volume)
        velocity = velocity + time_step * forces / inertia
        displacement = displacement + time_step * velocity
    return (displacement, velocity, forces)
```

```python
import functools
import math

import jax
import jax.numpy as jnp
from jax import lax
from jax.experimental import pallas as pl
from jax.experimental.pallas import tpu as pltpu
from jax.sharding import PartitionSpec as P

STEPS = 2
TIME_STEP = 0.02
F32 = jnp.float32
CLASSES = 8

OFFSETS = [
    (a, b, c)
    for a in range(-3, 4)
    for b in range(-3, 4)
    for c in range(-3, 4)
    if a * a + b * b + c * c <= 9 and (a, b, c) > (0, 0, 0)
]
INDEX = {offset: k for k, offset in enumerate(OFFSETS)}
VOLUME = 2.0 * sum(math.sqrt(float(a * a + b * b + c * c)) for a, b, c in OFFSETS)


def directed(b):
    return [
        (a, c)
        for a in range(-3, 4)
        for c in range(-3, 4)
        if 0 < a * a + b * b + c * c <= 9
    ]


FLAG_BASE, _row = [], 0
for _a, _b, _c in OFFSETS:
    FLAG_BASE.append(_row)
    _row += 8 * (8 + _a)
FLAG_ROWS = _row

X_FLAG, _row = {}, 96
for _k, (_a, _b, _c) in enumerate(OFFSETS):
    if _a:
        X_FLAG[_k] = _row
        _row += 8 * _a
X_UP_ROWS, X_DOWN_ROWS = _row, 96

Y_SUM, Y_MATERIAL, Y_FLAGS = 144, 168, 216
Y_UP_FLAG, Y_DOWN_FLAG, _up, _down = {}, {}, Y_FLAGS, Y_FLAGS
for _k, (_a, _b, _c) in enumerate(OFFSETS):
    if _b > 0:
        Y_UP_FLAG[_k] = _up
        _up += _b * (8 + _a)
    elif _b < 0:
        Y_DOWN_FLAG[_k] = _down
        _down += -_b * (8 + _a)
Y_UP_ROWS, Y_DOWN_ROWS = -(-_up // 8) * 8, -(-_down // 8) * 8


def rows(start, count=8):
    return pl.ds(start, count)


def copy_rows(target, to, source, at, count):
    done = 0
    while done < count:
        size = min(8, count - done)
        target[rows(to + done, size), :] = source[rows(at + done, size), :]
        done += size


def roll(value, shift):
    return value if shift % 128 == 0 else pltpu.roll(value, shift % 128, 1)


def pack_first(u, material, intact, up, down):
    for n in range(3):
        up[24 * n : 24 * n + 24, :] = u[64 * n + 40 : 64 * n + 64, :]
        down[24 * n : 24 * n + 24, :] = u[64 * n : 64 * n + 24, :]
    up[72:96, :] = material[40:64, :].astype(F32)
    down[72:96, :] = material[0:24, :].astype(F32)
    for k, base in X_FLAG.items():
        a = OFFSETS[k][0]
        up[base : base + 8 * a, :] = intact[64 * k + 64 - 8 * a : 64 * k + 64, :].astype(F32)


def widen(target, base, own, own_base, below, above, at):
    for x in range(-3, 11):
        if x < 0:
            tile = below[at + 8 * (x + 3) : at + 8 * (x + 3) + 8, :]
        elif x < 8:
            tile = own[own_base + 8 * x : own_base + 8 * x + 8, :].astype(F32)
        else:
            tile = above[at + 8 * (x - 8) : at + 8 * (x - 8) + 8, :]
        target[pl.ds(base + x + 3, 8, stride=16), :] = tile
    for x in (14, 15):
        target[pl.ds(base + x, 8, stride=16), :] = jnp.zeros((8, 128), F32)


def shifted_row(field, fields, c, column):
    return ((c + 3) * fields + field) * 224 + (column + 3) * 16


def store_shifts(target, field, fields, column, half, tile, along_z):
    for c in range(-3, 4):
        value = roll(tile, -c)
        if along_z and c:
            value = value + float(c)
        target[rows(shifted_row(field, fields, c, column) + 8 * half), :] = value


def pair_geometry(shifts, fields, column, a, c, own_x, own_y, own_z):
    at = 3 + a
    x = shifts[rows(shifted_row(0, fields, c, column) + at), :] - own_x
    y = shifts[rows(shifted_row(1, fields, c, column) + at), :] - own_y
    z = shifts[rows(shifted_row(2, fields, c, column) + at), :] - own_z
    return x, y, z, x * x + y * y + z * z


def band_sum(flags, incoming, shifts, sums):
    def column_sum(y, carry):
        own = [shifts[rows(shifted_row(n, 3, 0, y) + 3), :] for n in range(3)]
        total = jnp.zeros((8, 128), F32)
        own_x = {a: own[0] - float(a) for a in range(-3, 4)}
        for b in range(-3, 4):
            own_y = own[1] - float(b)
            part = None
            for a, c in directed(b):
                _, _, _, square = pair_geometry(shifts, 3, y + b, a, c, own_x[a], own_y, own[2])
                length = square * lax.rsqrt(square)
                stretch = length - math.sqrt(float(a * a + b * b + c * c))
                if (a, b, c) > (0, 0, 0):
                    flag = flags[rows(FLAG_BASE[INDEX[a, b, c]] + y * (8 + a) + a), :]
                else:
                    flag = incoming[rows((INDEX[-a, -b, -c] * 14 + y + b + 3) * 8), :]
                part = flag * stretch if part is None else part + flag * stretch
            if b:
                inside = jnp.logical_and(y + b >= 0, y + b < 8)
                part = jnp.where(inside, part, 0.0)
            total = total + part
        sums[rows(8 * y), :] = total
        return carry

    lax.fori_loop(0, 8, column_sum, 0)


def own_shifts(wide, shifts):
    def column(y, carry):
        for n in range(3):
            for half in range(2):
                tile = wide[rows(128 * n + 16 * y + 8 * half), :]
                store_shifts(shifts, n, 3, y, half, tile, n == 2)
        return carry

    lax.fori_loop(0, 8, column, 0)


def pack_y(wide, sums, up, down):
    for n in range(3):
        up[48 * n : 48 * n + 48, :] = wide[128 * n + 80 : 128 * n + 128, :]
        down[48 * n : 48 * n + 48, :] = wide[128 * n : 128 * n + 48, :]
    up[Y_SUM : Y_SUM + 24, :] = sums[40:64, :]
    down[Y_SUM : Y_SUM + 24, :] = sums[0:24, :]


def band_first(
    place, u, material, intact, below, above, wide, wide_material, flags, incoming, sums, up, down, shifts
):
    last_x = jnp.where(place[0] == 1, 0.0, 1.0)
    zero = place[3]
    for n in range(3):
        widen(wide, 128 * n, u, 64 * n, below, above, 24 * n)
    widen(wide_material, 0, material, 0, below, above, 72)
    own_shifts(wide, shifts)
    lane = lax.broadcasted_iota(jnp.int32, (8, 128), 1)
    column = lax.broadcasted_iota(jnp.int32, (8, 128), 0)
    first_column = jnp.where(place[1] == 1, 0, -8)
    last_column = jnp.where(place[2] == 1, 8, 16)
    for b in range(-3, 4):
        in_y = jnp.logical_and(column + b >= first_column, column + b < last_column)
        for c in range(-3, 4):
            inside = jnp.logical_and(in_y, jnp.logical_and(lane + c >= 0, lane + c < 128))
            valid = jnp.where(inside, 1.0, 0.0).astype(F32)
            leaving = valid * last_x
            for a in range(4):
                k = INDEX.get((a, b, c))
                if k is None:
                    continue
                step = 8 + a
                for x in range(8):
                    tile = intact[64 * k + 8 * x : 64 * k + 8 * x + 8, :].astype(F32)
                    tile = tile * (leaving if x + a >= 8 else valid)
                    flags[pl.ds(FLAG_BASE[k] + a + x, 8, stride=step), :] = tile
                for t in range(a):
                    tile = below[X_FLAG[k] + 8 * t : X_FLAG[k] + 8 * t + 8, :] * valid
                    flags[pl.ds(FLAG_BASE[k] + t, 8, stride=step), :] = tile

    def turn(y, carry):
        for k, (a, b, c) in enumerate(OFFSETS):
            tile = flags[rows(FLAG_BASE[k] + y * (8 + a)), :]
            incoming[rows((k * 14 + y + 3) * 8), :] = roll(tile, c)
        return carry

    lax.fori_loop(0, 8, turn, 0)
    band_sum(flags, incoming, shifts, sums)
    pack_y(wide, sums, up, down)
    up[Y_MATERIAL : Y_MATERIAL + 48, :] = wide_material[80:128, :]
    down[Y_MATERIAL : Y_MATERIAL + 48, :] = wide_material[0:48, :]
    for k, (a, b, c) in enumerate(OFFSETS):
        if b > 0:
            copy_rows(up, zero + Y_UP_FLAG[k], flags, zero + FLAG_BASE[k] + (8 - b) * (8 + a), b * (8 + a))
        elif b < 0:
            copy_rows(down, zero + Y_DOWN_FLAG[k], flags, zero + FLAG_BASE[k], -b * (8 + a))


def band_next(u, below, above, flags, incoming, wide, sums, up, down, shifts):
    for n in range(3):
        widen(wide, 128 * n, u, 64 * n, below, above, 24 * n)
    own_shifts(wide, shifts)
    band_sum(flags, incoming, shifts, sums)
    pack_y(wide, sums, up, down)


def wide_tile(wide, before, after, field, column, half):
    if column < 0:
        return before[rows(48 * field + 16 * (column + 3) + 8 * half), :]
    if column < 8:
        return wide[rows(128 * field + 16 * column + 8 * half), :]
    return after[rows(48 * field + 16 * (column - 8) + 8 * half), :]


def strip_theta(first, place, wide, flags, incoming, sums, before, after, before_flags, after_flags, *rest):
    if first:
        theta, up, down, all_incoming, shifts = rest
        own_incoming, incoming = incoming, all_incoming

        def keep(k, carry):
            copy_rows(incoming, (k * 14 + 3) * 8, own_incoming, (k * 14 + 3) * 8, 64)
            return carry

        lax.fori_loop(0, len(OFFSETS), keep, 0)
        zero = place[3]
        for k, (a, b, c) in enumerate(OFFSETS):
            for n in range(abs(b)):
                if b > 0:
                    tile = before_flags[rows(zero + Y_UP_FLAG[k] + n * (8 + a)), :]
                    incoming[rows((k * 14 + 3 - b + n) * 8), :] = roll(tile, c)
                else:
                    tile = after_flags[rows(zero + Y_DOWN_FLAG[k] + n * (8 + a)), :]
                    incoming[rows((k * 14 + 11 + n) * 8), :] = roll(tile, c)
    else:
        theta, up, down, shifts = rest
        zero = place[3]
    for column in (-3, -2, -1, 0, 1, 2, 5, 6, 7, 8, 9, 10):
        for n in range(3):
            for half in range(2):
                tile = wide_tile(wide, before, after, n, column, half)
                store_shifts(shifts, n, 3, column, half, tile, n == 2)
    for column in range(-3, 11):
        if column < 0:
            total = before[rows(Y_SUM + 8 * (column + 3)), :]
            partners = range(-column, 4)
        elif column < 8:
            total = sums[rows(8 * column), :]
            partners = [b for b in range(-3, 4) if not 0 <= column + b < 8]
        else:
            total = after[rows(Y_SUM + 8 * (column - 8)), :]
            partners = range(-3, 8 - column)
        own = [shifts[rows(zero + shifted_row(n, 3, 0, column) + 3), :] for n in range(3)] if len(partners) else None
        for b in partners:
            own_y = own[1] - float(b)
            for a, c in directed(b):
                own_x = own[0] - float(a)
                _, _, _, square = pair_geometry(shifts, 3, zero * 0 + column + b, a, c, own_x, own_y, own[2])
                length = square * lax.rsqrt(square)
                stretch = length - math.sqrt(float(a * a + b * b + c * c))
                if (a, b, c) > (0, 0, 0):
                    k = INDEX[a, b, c]
                    if column < 0:
                        flag = before_flags[rows(zero + Y_UP_FLAG[k] + (column + b) * (8 + a) + a), :]
                    elif column < 8:
                        flag = flags[rows(zero + FLAG_BASE[k] + column * (8 + a) + a), :]
                    else:
                        flag = after_flags[rows(zero + Y_DOWN_FLAG[k] + (column - 8) * (8 + a) + a), :]
                else:
                    flag = incoming[rows((INDEX[-a, -b, -c] * 14 + column + b + 3) * 8), :]
                total = total + flag * stretch
        theta[rows(8 * (column + 3)), :] = total
        up[rows(zero + 3 * (column + 3), 3), :] = theta[rows(zero + 8 * (column + 3) + 5, 3), :]
        down[rows(zero + 3 * (column + 3), 3), :] = theta[rows(zero + 8 * (column + 3), 3), :]


def pick(numbers, values):
    result = jnp.full(numbers.shape, values[CLASSES - 1], F32)
    for n in range(CLASSES - 1):
        result = jnp.where(numbers == float(n), values[n], result)
    return result


def advance(last, place, bulk, shear, density, u, v, wide, before, after, wide_material, before_material, after_material,
            theta, below, above, flags, incoming, *rest):
    if last:
        new_u, new_v, force, shifts, wide_theta = rest
    else:
        new_u, new_v, up, down, shifts, wide_theta = rest
        force = None
    zero = place[3]
    twist = [shear[n] * (15.0 / VOLUME) for n in range(CLASSES)]
    press = [(bulk[n] * 3.0 - shear[n] * 5.0) * (3.0 / (VOLUME * VOLUME)) for n in range(CLASSES)]
    inertia = [density[n] for n in range(CLASSES)]
    for column in range(-3, 11):
        at = 16 * (column + 3)
        wide_theta[rows(zero + at + 3), :] = theta[8 * (column + 3) : 8 * (column + 3) + 8, :]
        wide_theta[rows(zero + at, 3), :] = below[rows(zero + 3 * (column + 3), 3), :]
        wide_theta[rows(zero + at + 11, 3), :] = above[rows(zero + 3 * (column + 3), 3), :]
        wide_theta[rows(zero + at + 14, 2), :] = jnp.zeros((2, 128), F32)
        for half in range(2):
            for n in range(3):
                tile = wide_tile(wide, before, after, n, column, half)
                store_shifts(shifts, n, 5, column, half, tile, n == 2)
            if column < 0:
                number = before_material[rows(Y_MATERIAL + 16 * (column + 3) + 8 * half), :]
            elif column < 8:
                number = wide_material[rows(16 * column + 8 * half), :]
            else:
                number = after_material[rows(Y_MATERIAL + 16 * (column - 8) + 8 * half), :]
            twisting = pick(number, twist)
            pressing = pick(number, press) * wide_theta[rows(at + 8 * half), :] - twisting
            store_shifts(shifts, 3, 5, column, half, pressing, False)
            store_shifts(shifts, 4, 5, column, half, twisting, False)

    def column_force(y, carry):
        own = [shifts[rows(shifted_row(n, 5, 0, y) + 3), :] for n in range(5)]
        own_x = {a: own[0] - float(a) for a in range(-3, 4)}
        total = [jnp.zeros((8, 128), F32) for _ in range(3)]
        for b in range(-3, 4):
            own_y = own[1] - float(b)
            for a, c in directed(b):
                *vector, square = pair_geometry(shifts, 5, y + b, a, c, own_x[a], own_y, own[2])
                inverse = lax.rsqrt(square)
                pressing = shifts[rows(shifted_row(3, 5, c, y + b) + 3 + a), :] + own[3]
                twisting = shifts[rows(shifted_row(4, 5, c, y + b) + 3 + a), :] + own[4]
                if (a, b, c) > (0, 0, 0):
                    flag = flags[rows(FLAG_BASE[INDEX[a, b, c]] + y * (8 + a) + a), :]
                else:
                    flag = incoming[rows((INDEX[-a, -b, -c] * 14 + y + b + 3) * 8), :]
                size = flag * (pressing * inverse + twisting * (1.0 / math.sqrt(float(a * a + b * b + c * c))))
                total = [t + size * w for t, w in zip(total, vector)]
        number = wide_material[rows(16 * y + 3), :]
        mass = pick(number, inertia)
        for n in range(3):
            at = pl.ds(64 * n + y, 8, stride=8)
            speed = v[at, :] + TIME_STEP * total[n] / mass
            new_v[at, :] = speed
            new_u[at, :] = u[at, :] + TIME_STEP * speed
            if last:
                force[at, :] = total[n]
        return carry

    lax.fori_loop(0, 8, column_force, 0)
    if not last:
        for n in range(3):
            up[24 * n : 24 * n + 24, :] = new_u[64 * n + 40 : 64 * n + 64, :]
            down[24 * n : 24 * n + 24, :] = new_u[64 * n : 64 * n + 24, :]


VMEM = pl.BlockSpec(memory_space=pltpu.VMEM)
SMEM = pl.BlockSpec(memory_space=pltpu.SMEM)


def call(body, outputs, scratch, scalars, *arguments, flops=0):
    shapes = [jax.ShapeDtypeStruct((n, 128), F32) for n in outputs]
    traffic = 512 * sum(outputs) + sum(4 * x.size for x in arguments)
    return pl.pallas_call(
        body,
        out_shape=shapes,
        in_specs=[SMEM] * scalars + [VMEM] * (len(arguments) - scalars),
        out_specs=[VMEM] * len(shapes),
        scratch_shapes=[pltpu.VMEM((n, 128), F32) for n in scratch],
        compiler_params=pltpu.CompilerParams(vmem_limit_bytes=24 << 20),
        cost_estimate=pl.CostEstimate(flops=flops, bytes_accessed=traffic, transcendentals=0),
    )(*arguments)


def both_ways(up, down, axis):
    size = lax.axis_size(axis)
    route = [(i, i + 1) for i in range(size - 1)]
    from_below = lax.ppermute(up, axis, route)
    from_above = lax.ppermute(down, axis, [(j, i) for i, j in route])
    return from_below, from_above


def on_device(displacement, velocity, intact, material, bulk_modulus, shear_modulus, density):
    shape = displacement.shape
    u, v = displacement.reshape(192, 128), velocity.reshape(192, 128)
    flags_in = intact.reshape(len(OFFSETS) * 64, 128)
    material = material.reshape(64, 128)
    gx, gy = lax.axis_index("gx"), lax.axis_index("gy")
    place = jnp.stack(
        [gx == lax.axis_size("gx") - 1, gy == 0, gy == lax.axis_size("gy") - 1, gy < 0]
    ).astype(jnp.int32)
    tables = (bulk_modulus, shear_modulus, density)
    all_rows = len(OFFSETS) * 14 * 8
    up, down = call(pack_first, [X_UP_ROWS, X_DOWN_ROWS], [], 0, u, material, flags_in)
    below, above = both_ways(up, down, "gx")
    wide, wide_material, flags, incoming, sums, up, down = call(
        band_first,
        [384, 128, FLAG_ROWS, all_rows, 64, Y_UP_ROWS, Y_DOWN_ROWS],
        [7 * 3 * 224],
        1, place, u, material, flags_in, below, above,
    )
    before, after = both_ways(up, down, "gy")
    first_before, first_after = before, after
    for step in range(STEPS):
        if step:
            below, above = both_ways(up, down, "gx")
            wide, sums, up, down = call(
                band_next, [384, 64, Y_FLAGS, Y_FLAGS], [7 * 3 * 224], 0, u, below, above, flags, incoming
            )
            before, after = both_ways(up, down, "gy")
        outputs = [112, 48, 48] + ([] if step else [all_rows])
        theta, up, down, *more = call(
            functools.partial(strip_theta, step == 0), outputs, [7 * 3 * 224],
            1, place, wide, flags, incoming, sums, before, after, first_before, first_after,
        )
        if not step:
            incoming = more[0]
        below, above = both_ways(up, down, "gx")
        last = step == STEPS - 1
        u, v, *more = call(
            functools.partial(advance, last), [192, 192] + ([192] if last else [72, 72]), [7 * 5 * 224, 224],
            4, place, *tables, u, v, wide, before, after, wide_material, first_before, first_after,
            theta, below, above, flags, incoming,
        )
        if last:
            force = more[0]
        else:
            up, down = more
    return u.reshape(shape), v.reshape(shape), force.reshape(shape)


def solution(mesh):
    return jax.shard_map(
        on_device,
        mesh=mesh,
        in_specs=(
            P(None, "gx", "gy", None),
            P(None, "gx", "gy", None),
            P(None, "gx", "gy", None),
            P("gx", "gy", None),
            P(),
            P(),
            P(),
        ),
        out_specs=(P(None, "gx", "gy", None), P(None, "gx", "gy", None), P(None, "gx", "gy", None)),
        check_vma=False,
    )
```

```python
import functools
import math

import jax
import jax.numpy as jnp
from jax import lax
from jax.experimental import pallas as pl
from jax.experimental.pallas import tpu as pltpu
from jax.sharding import PartitionSpec as P

STEPS = 2
TIME_STEP = 0.02
F32 = jnp.float32
CLASSES = 8

OFFSETS = [
    (a, b, c)
    for a in range(-3, 4)
    for b in range(-3, 4)
    for c in range(-3, 4)
    if a * a + b * b + c * c <= 9 and (a, b, c) > (0, 0, 0)
]
INDEX = {offset: k for k, offset in enumerate(OFFSETS)}
VOLUME = 2.0 * sum(math.sqrt(float(a * a + b * b + c * c)) for a, b, c in OFFSETS)


def directed(b):
    return [
        (a, c)
        for a in range(-3, 4)
        for c in range(-3, 4)
        if 0 < a * a + b * b + c * c <= 9
    ]


FLAG_BASE, _row = [], 0
for _a, _b, _c in OFFSETS:
    FLAG_BASE.append(_row)
    _row += 8 * (8 + _a)
FLAG_ROWS = _row

X_FLAG, _row = {}, 96
for _k, (_a, _b, _c) in enumerate(OFFSETS):
    if _a:
        X_FLAG[_k] = _row
        _row += 8 * _a
X_UP_ROWS, X_DOWN_ROWS = _row, 96

Y_SUM, Y_MATERIAL, Y_FLAGS = 144, 168, 216
Y_UP_FLAG, Y_DOWN_FLAG, _up, _down = {}, {}, Y_FLAGS, Y_FLAGS
for _k, (_a, _b, _c) in enumerate(OFFSETS):
    if _b > 0:
        Y_UP_FLAG[_k] = _up
        _up += _b * (8 + _a)
    elif _b < 0:
        Y_DOWN_FLAG[_k] = _down
        _down += -_b * (8 + _a)
Y_UP_ROWS, Y_DOWN_ROWS = -(-_up // 8) * 8, -(-_down // 8) * 8


def rows(start, count=8):
    return pl.ds(start, count)


def copy_rows(target, to, source, at, count):
    done = 0
    while done < count:
        size = min(8, count - done)
        target[rows(to + done, size), :] = source[rows(at + done, size), :]
        done += size


def roll(value, shift):
    return value if shift % 128 == 0 else pltpu.roll(value, shift % 128, 1)


def place_messages(even, up, down, far, near):
    near[...] = jnp.where(even, up[...], down[...])
    far[...] = jnp.where(even, down[...], up[...])


def take_messages(even, first, last, far, near, below, above):
    size = above.shape[0]
    below[...] = jnp.where(first, 0.0, jnp.where(even, far[...], near[...]))
    above[...] = jnp.where(last, 0.0, jnp.where(even, near[0:size, :], far[0:size, :]))


def place_along_x(place, *blocks):
    place_messages(place[4] == 1, *blocks)


def place_along_y(place, *blocks):
    place_messages(place[6] == 1, *blocks)


def take_along_x(place, *blocks):
    take_messages(place[4] == 1, place[5] == 1, place[0] == 1, *blocks)


def take_along_y(place, *blocks):
    take_messages(place[6] == 1, place[1] == 1, place[2] == 1, *blocks)


def pack_first(place, u_in, material_in, intact_in, near, far, u, material, material_copy, ones, twos, threes, up, down, done):
    parts = [
        pltpu.make_async_copy(u_in, u, done.at[0]),
        pltpu.make_async_copy(material_in, material_copy, done.at[1]),
    ]
    for a, block in ((1, ones), (2, twos), (3, threes)):
        first = min(k for k in X_FLAG if OFFSETS[k][0] == a)
        source = intact_in.at[pl.ds(first, block.shape[0]), pl.ds(64 - 8 * a, 8 * a), :]
        parts.append(pltpu.make_async_copy(source, block, done.at[1 + a]))
    for part in parts:
        part.start()
    for part in parts:
        part.wait()
    for n in range(3):
        up[24 * n : 24 * n + 24, :] = u[64 * n + 40 : 64 * n + 64, :]
        down[24 * n : 24 * n + 24, :] = u[64 * n : 64 * n + 24, :]
    material[...] = material_copy[...].astype(F32)
    up[72:96, :] = material_copy[40:64, :].astype(F32)
    down[72:96, :] = material_copy[0:24, :].astype(F32)
    at = 96
    for block in (ones, twos, threes):
        size = block.shape[0] * block.shape[1]
        up[at : at + size, :] = block[...].astype(F32).reshape(size, 128)
        at += size
    place_along_x(place, up, down, near, far)


def widen(target, base, own, own_base, below, above, at):
    for x in range(-3, 11):
        if x < 0:
            tile = below[at + 8 * (x + 3) : at + 8 * (x + 3) + 8, :]
        elif x < 8:
            tile = own[own_base + 8 * x : own_base + 8 * x + 8, :]
        else:
            tile = above[at + 8 * (x - 8) : at + 8 * (x - 8) + 8, :]
        target[pl.ds(base + x + 3, 8, stride=16), :] = tile
    for x in (14, 15):
        target[pl.ds(base + x, 8, stride=16), :] = jnp.zeros((8, 128), F32)


def shifted_row(field, fields, c, column):
    return ((c + 3) * fields + field) * 224 + (column + 3) * 16


def store_shifts(target, field, fields, column, half, tile, along_z):
    for c in range(-3, 4):
        value = roll(tile, -c)
        if along_z and c:
            value = value + float(c)
        target[rows(shifted_row(field, fields, c, column) + 8 * half), :] = value


def pair_geometry(shifts, fields, column, a, c, own_x, own_y, own_z):
    at = 3 + a
    x = shifts[rows(shifted_row(0, fields, c, column) + at), :] - own_x
    y = shifts[rows(shifted_row(1, fields, c, column) + at), :] - own_y
    z = shifts[rows(shifted_row(2, fields, c, column) + at), :] - own_z
    return x, y, z, x * x + y * y + z * z


def band_sum(flags, incoming, shifts, sums):
    def column_sum(y, carry):
        own = [shifts[rows(shifted_row(n, 3, 0, y) + 3), :] for n in range(3)]
        total = jnp.zeros((8, 128), F32)
        own_x = {a: own[0] - float(a) for a in range(-3, 4)}
        for b in range(-3, 4):
            own_y = own[1] - float(b)
            part = None
            for a, c in directed(b):
                _, _, _, square = pair_geometry(shifts, 3, y + b, a, c, own_x[a], own_y, own[2])
                length = square * lax.rsqrt(square)
                stretch = length - math.sqrt(float(a * a + b * b + c * c))
                if (a, b, c) > (0, 0, 0):
                    flag = flags[rows(FLAG_BASE[INDEX[a, b, c]] + y * (8 + a) + a), :]
                else:
                    flag = incoming[rows((INDEX[-a, -b, -c] * 14 + y + b + 3) * 8), :]
                part = flag * stretch if part is None else part + flag * stretch
            if b:
                inside = jnp.logical_and(y + b >= 0, y + b < 8)
                part = jnp.where(inside, part, 0.0)
            total = total + part
        sums[rows(8 * y), :] = total
        return carry

    lax.fori_loop(0, 8, column_sum, 0)


def own_shifts(wide, shifts):
    def column(y, carry):
        for n in range(3):
            for half in range(2):
                tile = wide[rows(128 * n + 16 * y + 8 * half), :]
                store_shifts(shifts, n, 3, y, half, tile, n == 2)
        return carry

    lax.fori_loop(0, 8, column, 0)


def pack_y(wide, sums, up, down):
    for n in range(3):
        up[48 * n : 48 * n + 48, :] = wide[128 * n + 80 : 128 * n + 128, :]
        down[48 * n : 48 * n + 48, :] = wide[128 * n : 128 * n + 48, :]
    up[Y_SUM : Y_SUM + 24, :] = sums[40:64, :]
    down[Y_SUM : Y_SUM + 24, :] = sums[0:24, :]


def validity(place, b, c):
    lane = lax.broadcasted_iota(jnp.int32, (8, 128), 1)
    column = lax.broadcasted_iota(jnp.int32, (8, 128), 0)
    first_column = jnp.where(place[1] == 1, 0, -8)
    last_column = jnp.where(place[2] == 1, 8, 16)
    in_y = jnp.logical_and(column + b >= first_column, column + b < last_column)
    inside = jnp.logical_and(in_y, jnp.logical_and(lane + c >= 0, lane + c < 128))
    return jnp.where(inside, 1.0, 0.0).astype(F32)


def prepare_flags(place, intact, flags, incoming):
    last_x = jnp.where(place[0] == 1, 0.0, 1.0)
    for b in range(-3, 4):
        for c in range(-3, 4):
            valid = validity(place, b, c)
            leaving = valid * last_x
            for a in range(4):
                k = INDEX.get((a, b, c))
                if k is None:
                    continue
                for x in range(8):
                    tile = intact[64 * k + 8 * x : 64 * k + 8 * x + 8, :].astype(F32)
                    tile = tile * (leaving if x + a >= 8 else valid)
                    flags[pl.ds(FLAG_BASE[k] + a + x, 8, stride=8 + a), :] = tile

    def turn(y, carry):
        for k, (a, b, c) in enumerate(OFFSETS):
            tile = flags[rows(FLAG_BASE[k] + y * (8 + a)), :]
            incoming[rows((k * 14 + y + 3) * 8), :] = roll(tile, c)
        return carry

    lax.fori_loop(0, 8, turn, 0)


def band_first(
    place, u, material, near, far, own_flags, own_incoming,
    wide, wide_material, sums, near_y, far_y, flags, incoming, shifts, below, above, up, down,
):
    zero = place[3]
    take_along_x(place, near, far, below, above)
    for k, base in X_FLAG.items():
        a, b, c = OFFSETS[k]
        valid = validity(place, b, c)
        for t in range(a):
            tile = below[base + 8 * t : base + 8 * t + 8, :] * valid
            flags[pl.ds(FLAG_BASE[k] + t, 8, stride=8 + a), :] = tile
            incoming[pl.ds((k * 14 + 3) * 8 + t, 8, stride=8), :] = roll(tile, c)
    for n in range(3):
        widen(wide, 128 * n, u, 64 * n, below, above, 24 * n)
    widen(wide_material, 0, material, 0, below, above, 72)
    own_shifts(wide, shifts)
    band_sum(flags, incoming, shifts, sums)
    pack_y(wide, sums, up, down)
    up[Y_MATERIAL : Y_MATERIAL + 48, :] = wide_material[80:128, :]
    down[Y_MATERIAL : Y_MATERIAL + 48, :] = wide_material[0:48, :]
    for k, (a, b, c) in enumerate(OFFSETS):
        if b > 0:
            copy_rows(up, zero + Y_UP_FLAG[k], flags, zero + FLAG_BASE[k] + (8 - b) * (8 + a), b * (8 + a))
        elif b < 0:
            copy_rows(down, zero + Y_DOWN_FLAG[k], flags, zero + FLAG_BASE[k], -b * (8 + a))
    place_along_y(place, up, down, near_y, far_y)


def band_next(
    place, u, near, far, flags, incoming, wide, sums, near_y, far_y, shifts, below, above, up, down
):
    take_along_x(place, near, far, below, above)
    for n in range(3):
        widen(wide, 128 * n, u, 64 * n, below, above, 24 * n)
    own_shifts(wide, shifts)
    band_sum(flags, incoming, shifts, sums)
    pack_y(wide, sums, up, down)
    place_along_y(place, up, down, near_y, far_y)


def wide_tile(wide, before, after, field, column, half):
    if column < 0:
        return before[rows(48 * field + 16 * (column + 3) + 8 * half), :]
    if column < 8:
        return wide[rows(128 * field + 16 * column + 8 * half), :]
    return after[rows(48 * field + 16 * (column - 8) + 8 * half), :]


def strip_theta(first, place, wide, flags, incoming, sums, near, far, *rest):
    if not first:
        before_flags, after_flags, *rest = rest
    theta, near_x, far_x, before, after, *rest = rest
    take_along_y(place, near, far, before, after)
    if first:
        all_incoming, shifts, up, down = rest
        before_flags, after_flags = before, after
        own_incoming, incoming = incoming, all_incoming

        def keep(k, carry):
            copy_rows(incoming, (k * 14 + 3) * 8, own_incoming, (k * 14 + 3) * 8, 64)
            return carry

        lax.fori_loop(0, len(OFFSETS), keep, 0)
        zero = place[3]
        for k, (a, b, c) in enumerate(OFFSETS):
            for n in range(abs(b)):
                if b > 0:
                    tile = before_flags[rows(zero + Y_UP_FLAG[k] + n * (8 + a)), :]
                    incoming[rows((k * 14 + 3 - b + n) * 8), :] = roll(tile, c)
                else:
                    tile = after_flags[rows(zero + Y_DOWN_FLAG[k] + n * (8 + a)), :]
                    incoming[rows((k * 14 + 11 + n) * 8), :] = roll(tile, c)
    else:
        shifts, up, down = rest
        zero = place[3]
    for column in (-3, -2, -1, 0, 1, 2, 5, 6, 7, 8, 9, 10):
        for n in range(3):
            for half in range(2):
                tile = wide_tile(wide, before, after, n, column, half)
                store_shifts(shifts, n, 3, column, half, tile, n == 2)
    for block in (up, down):
        block[40:48, :] = jnp.zeros((8, 128), F32)
    for column in range(-3, 11):
        if column < 0:
            total = before[rows(Y_SUM + 8 * (column + 3)), :]
            partners = range(-column, 4)
        elif column < 8:
            total = sums[rows(8 * column), :]
            partners = [b for b in range(-3, 4) if not 0 <= column + b < 8]
        else:
            total = after[rows(Y_SUM + 8 * (column - 8)), :]
            partners = range(-3, 8 - column)
        own = [shifts[rows(zero + shifted_row(n, 3, 0, column) + 3), :] for n in range(3)] if len(partners) else None
        for b in partners:
            own_y = own[1] - float(b)
            for a, c in directed(b):
                own_x = own[0] - float(a)
                _, _, _, square = pair_geometry(shifts, 3, zero * 0 + column + b, a, c, own_x, own_y, own[2])
                length = square * lax.rsqrt(square)
                stretch = length - math.sqrt(float(a * a + b * b + c * c))
                if (a, b, c) > (0, 0, 0):
                    k = INDEX[a, b, c]
                    if column < 0:
                        flag = before_flags[rows(zero + Y_UP_FLAG[k] + (column + b) * (8 + a) + a), :]
                    elif column < 8:
                        flag = flags[rows(zero + FLAG_BASE[k] + column * (8 + a) + a), :]
                    else:
                        flag = after_flags[rows(zero + Y_DOWN_FLAG[k] + (column - 8) * (8 + a) + a), :]
                else:
                    flag = incoming[rows((INDEX[-a, -b, -c] * 14 + column + b + 3) * 8), :]
                total = total + flag * stretch
        theta[rows(8 * (column + 3)), :] = total
        up[rows(zero + 3 * (column + 3), 3), :] = theta[rows(zero + 8 * (column + 3) + 5, 3), :]
        down[rows(zero + 3 * (column + 3), 3), :] = theta[rows(zero + 8 * (column + 3), 3), :]
    place_along_x(place, up, down, near_x, far_x)


def pick(numbers, values):
    result = jnp.full(numbers.shape, values[CLASSES - 1], F32)
    for n in range(CLASSES - 1):
        result = jnp.where(numbers == float(n), values[n], result)
    return result


def advance(last, place, bulk, shear, density, u, v, wide, before, after, wide_material, before_material, after_material,
            theta, near, far, flags, incoming, *rest):
    if last:
        new_u, new_v, force, shifts, wide_theta, below, above = rest
    else:
        new_u, new_v, near_x, far_x, shifts, wide_theta, below, above, up, down = rest
        force = None
    zero = place[3]
    take_along_x(place, near, far, below, above)
    twist = [shear[n] * (15.0 / VOLUME) for n in range(CLASSES)]
    press = [(bulk[n] * 3.0 - shear[n] * 5.0) * (3.0 / (VOLUME * VOLUME)) for n in range(CLASSES)]
    inertia = [density[n] for n in range(CLASSES)]
    for column in range(-3, 11):
        at = 16 * (column + 3)
        wide_theta[rows(zero + at + 3), :] = theta[8 * (column + 3) : 8 * (column + 3) + 8, :]
        wide_theta[rows(zero + at, 3), :] = below[rows(zero + 3 * (column + 3), 3), :]
        wide_theta[rows(zero + at + 11, 3), :] = above[rows(zero + 3 * (column + 3), 3), :]
        wide_theta[rows(zero + at + 14, 2), :] = jnp.zeros((2, 128), F32)
        for half in range(2):
            for n in range(3):
                tile = wide_tile(wide, before, after, n, column, half)
                store_shifts(shifts, n, 5, column, half, tile, n == 2)
            if column < 0:
                number = before_material[rows(Y_MATERIAL + 16 * (column + 3) + 8 * half), :]
            elif column < 8:
                number = wide_material[rows(16 * column + 8 * half), :]
            else:
                number = after_material[rows(Y_MATERIAL + 16 * (column - 8) + 8 * half), :]
            twisting = pick(number, twist)
            pressing = pick(number, press) * wide_theta[rows(at + 8 * half), :] - twisting
            store_shifts(shifts, 3, 5, column, half, pressing, False)
            store_shifts(shifts, 4, 5, column, half, twisting, False)

    def column_force(y, carry):
        own = [shifts[rows(shifted_row(n, 5, 0, y) + 3), :] for n in range(5)]
        own_x = {a: own[0] - float(a) for a in range(-3, 4)}
        total = [jnp.zeros((8, 128), F32) for _ in range(3)]
        for b in range(-3, 4):
            own_y = own[1] - float(b)
            for a, c in directed(b):
                *vector, square = pair_geometry(shifts, 5, y + b, a, c, own_x[a], own_y, own[2])
                inverse = lax.rsqrt(square)
                pressing = shifts[rows(shifted_row(3, 5, c, y + b) + 3 + a), :] + own[3]
                twisting = shifts[rows(shifted_row(4, 5, c, y + b) + 3 + a), :] + own[4]
                if (a, b, c) > (0, 0, 0):
                    flag = flags[rows(FLAG_BASE[INDEX[a, b, c]] + y * (8 + a) + a), :]
                else:
                    flag = incoming[rows((INDEX[-a, -b, -c] * 14 + y + b + 3) * 8), :]
                size = flag * (pressing * inverse + twisting * (1.0 / math.sqrt(float(a * a + b * b + c * c))))
                total = [t + size * w for t, w in zip(total, vector)]
        number = wide_material[rows(16 * y + 3), :]
        mass = pick(number, inertia)
        for n in range(3):
            at = pl.ds(64 * n + y, 8, stride=8)
            speed = v[at, :] + TIME_STEP * total[n] / mass
            new_v[at, :] = speed
            new_u[at, :] = u[at, :] + TIME_STEP * speed
            if last:
                force[at, :] = total[n]
        return carry

    lax.fori_loop(0, 8, column_force, 0)
    if not last:
        for n in range(3):
            up[24 * n : 24 * n + 24, :] = new_u[64 * n + 40 : 64 * n + 64, :]
            down[24 * n : 24 * n + 24, :] = new_u[64 * n : 64 * n + 24, :]
        place_along_x(place, up, down, near_x, far_x)


VMEM = pl.BlockSpec(memory_space=pltpu.VMEM)
SMEM = pl.BlockSpec(memory_space=pltpu.SMEM)
IN_HBM = pl.BlockSpec(memory_space=pltpu.HBM)


def call(body, outputs, scratch, scalars, *arguments, flops=0, aliases={}, place=VMEM, limit=24):
    shapes = [jax.ShapeDtypeStruct((n, 128), F32) for n in outputs]
    traffic = 512 * sum(outputs) + sum(4 * x.size for x in arguments)
    return pl.pallas_call(
        body,
        out_shape=shapes,
        in_specs=[SMEM] * scalars + [place] * (len(arguments) - scalars),
        out_specs=[VMEM] * len(shapes),
        scratch_shapes=[pltpu.VMEM((n, 128), F32) if isinstance(n, int) else n for n in scratch],
        input_output_aliases=aliases,
        compiler_params=pltpu.CompilerParams(vmem_limit_bytes=limit << 20),
        cost_estimate=pl.CostEstimate(flops=flops, bytes_accessed=traffic, transcendentals=0),
    )(*arguments)


def swap_pairs(far, near, axis):
    sizes = {name: lax.axis_size(name) for name in ("gx", "gy")}
    other = "gy" if axis == "gx" else "gx"
    size = sizes[axis]

    def device(along, across):
        at = {axis: along, other: across}
        return at["gx"] * sizes["gy"] + at["gy"]

    swaps = []
    for start in (0, 1):
        pairs = []
        for across in range(sizes[other]):
            for along in range(size):
                partner = along + 1 if (along - start) % 2 == 0 else along - 1
                inside = 0 <= partner < size
                target = device(partner, across) if inside else device(along, across ^ 1)
                pairs.append((device(along, across), target))
        swaps.append(pairs)
    far = lax.ppermute(far, ("gx", "gy"), swaps[1])
    near = lax.ppermute(near, ("gx", "gy"), swaps[0])
    return far, near


def on_device(displacement, velocity, intact, material, bulk_modulus, shear_modulus, density):
    shape = displacement.shape
    bonds = len(OFFSETS)
    u, v = displacement.reshape(192, 128), velocity.reshape(192, 128)
    material = material.reshape(64, 128)
    gx, gy = lax.axis_index("gx"), lax.axis_index("gy")
    place = jnp.stack(
        [gx == lax.axis_size("gx") - 1, gy == 0, gy == lax.axis_size("gy") - 1, gy < 0, gx % 2 == 0, gx == 0, gy % 2 == 0]
    ).astype(jnp.int32)
    tables = (bulk_modulus, shear_modulus, density)
    all_rows = bonds * 14 * 8
    counts = [sum(offset[0] == a for offset in OFFSETS) for a in (1, 2, 3)]
    blocks = [pltpu.VMEM((count, 8 * a, 128), jnp.int32) for a, count in zip((1, 2, 3), counts)]
    far, near, u, material = call(
        pack_first, [X_UP_ROWS, X_UP_ROWS, 192, 64],
        [pltpu.VMEM((64, 128), jnp.int32), *blocks, X_UP_ROWS, X_UP_ROWS, pltpu.SemaphoreType.DMA((5,))],
        1, place, u, material, intact.reshape(bonds, 64, 128), place=IN_HBM,
    )
    flags, incoming = call(
        prepare_flags, [FLAG_ROWS, all_rows], [], 1, place, intact.reshape(bonds * 64, 128), flops=bonds * 8192 * 4
    )
    far, near = swap_pairs(far, near, "gx")
    wide, wide_material, sums, far, near, flags, incoming = call(
        band_first,
        [384, 128, 64, Y_UP_ROWS, Y_UP_ROWS, FLAG_ROWS, all_rows],
        [7 * 3 * 224, X_UP_ROWS, X_DOWN_ROWS, Y_UP_ROWS, Y_UP_ROWS],
        1, place, u, material, far, near, flags, incoming, aliases={5: 5, 6: 6},
    )
    far, near = swap_pairs(far, near, "gy")
    for step in range(STEPS):
        if step:
            far, near = swap_pairs(far, near, "gx")
            wide, sums, far, near = call(
                band_next, [384, 64, Y_MATERIAL, Y_MATERIAL], [7 * 3 * 224, 72, 72, Y_MATERIAL, Y_MATERIAL],
                1, place, u, far, near, flags, incoming,
            )
            far, near = swap_pairs(far, near, "gy")
            theta, far, near, before, after = call(
                functools.partial(strip_theta, False), [112, 48, 48, Y_MATERIAL, Y_MATERIAL], [7 * 3 * 224, 48, 48],
                1, place, wide, flags, incoming, sums, far, near, first_before, first_after,
            )
        else:
            theta, far, near, before, after, incoming = call(
                functools.partial(strip_theta, True), [112, 48, 48, Y_UP_ROWS, Y_UP_ROWS, all_rows],
                [7 * 3 * 224, 48, 48],
                1, place, wide, flags, incoming, sums, far, near,
            )
            first_before, first_after = before, after
        far, near = swap_pairs(far, near, "gx")
        last = step == STEPS - 1
        u, v, *more = call(
            functools.partial(advance, last), [192, 192] + ([192] if last else [72, 72]),
            [7 * 5 * 224, 224, 48, 48] + ([] if last else [72, 72]),
            4, place, *tables, u, v, wide, before, after, wide_material, first_before, first_after,
            theta, far, near, flags, incoming,
        )
        if last:
            force = more[0]
        else:
            far, near = more
    return u.reshape(shape), v.reshape(shape), force.reshape(shape)


def solution(mesh):
    return jax.shard_map(
        on_device,
        mesh=mesh,
        in_specs=(
            P(None, "gx", "gy", None),
            P(None, "gx", "gy", None),
            P(None, "gx", "gy", None),
            P("gx", "gy", None),
            P(),
            P(),
            P(),
        ),
        out_specs=(P(None, "gx", "gy", None), P(None, "gx", "gy", None), P(None, "gx", "gy", None)),
        check_vma=False,
    )
```

```python
import functools
import math

import jax
import jax.numpy as jnp
from jax import lax
from jax.experimental import pallas as pl
from jax.experimental.pallas import tpu as pltpu
from jax.sharding import PartitionSpec as P

STEPS = 2
TIME_STEP = 0.02
F32 = jnp.float32
CLASSES = 8

OFFSETS = [
    (a, b, c)
    for a in range(-3, 4)
    for b in range(-3, 4)
    for c in range(-3, 4)
    if a * a + b * b + c * c <= 9 and (a, b, c) > (0, 0, 0)
]
INDEX = {offset: k for k, offset in enumerate(OFFSETS)}
VOLUME = 2.0 * sum(math.sqrt(float(a * a + b * b + c * c)) for a, b, c in OFFSETS)


def directed(b):
    return [
        (a, c)
        for a in range(-3, 4)
        for c in range(-3, 4)
        if 0 < a * a + b * b + c * c <= 9
    ]


FLAG_BASE, _row = [], 0
for _a, _b, _c in OFFSETS:
    FLAG_BASE.append(_row)
    _row += 8 * (8 + _a)
FLAG_ROWS = _row

X_FLAG, _row = {}, 96
for _k, (_a, _b, _c) in enumerate(OFFSETS):
    if _a:
        X_FLAG[_k] = _row
        _row += 8 * _a
X_UP_ROWS, X_DOWN_ROWS = _row, 96

Y_SUM, Y_MATERIAL, Y_FLAGS = 144, 168, 216
Y_UP_FLAG, Y_DOWN_FLAG, _up, _down = {}, {}, Y_FLAGS, Y_FLAGS
for _k, (_a, _b, _c) in enumerate(OFFSETS):
    if _b > 0:
        Y_UP_FLAG[_k] = _up
        _up += _b * (8 + _a)
    elif _b < 0:
        Y_DOWN_FLAG[_k] = _down
        _down += -_b * (8 + _a)
Y_ROWS = -(-max(_up, _down) // 8) * 8

EARLY, CORNER = {}, {}
for _sign in (1, -1):
    _early, _corner = 0, Y_FLAGS
    for _k, (_a, _b, _c) in enumerate(OFFSETS):
        if _b * _sign > 0:
            EARLY[_k], CORNER[_k] = _early, _corner
            _early += abs(_b) * 8
            _corner += abs(_b) * _a
EARLY_ROWS = max(EARLY[k] + 8 * abs(OFFSETS[k][1]) for k in EARLY)
CORNER_ROWS = -(-max(CORNER[k] + abs(OFFSETS[k][1]) * OFFSETS[k][0] for k in CORNER) // 8) * 8


def rows(start, count=8):
    return pl.ds(start, count)


def copy_rows(target, to, source, at, count):
    done = 0
    while done < count:
        size = min(8, count - done)
        target[rows(to + done, size), :] = source[rows(at + done, size), :]
        done += size


def roll(value, shift):
    return value if shift % 128 == 0 else pltpu.roll(value, shift % 128, 1)


def position():
    gx, gy = lax.axis_index("gx"), lax.axis_index("gy")
    last_x, last_y = lax.axis_size("gx") - 1, lax.axis_size("gy") - 1
    flags = [gx == last_x, gy == 0, gy == last_y, gy < 0, gx % 2 == 0, gx == 0, gy % 2 == 0]
    return [jnp.where(flag, 1, 0) for flag in flags]


def place_messages(even, up, down, far, near):
    near[...] = jnp.where(even, up[...], down[...])
    far[...] = jnp.where(even, down[...], up[...])


def take_messages(even, first, last, far, near, below, above):
    size = above.shape[0]
    below[...] = jnp.where(first, 0.0, jnp.where(even, far[...], near[...]))
    above[...] = jnp.where(last, 0.0, jnp.where(even, near[0:size, :], far[0:size, :]))


def place_along_x(place, *blocks):
    place_messages(place[4] == 1, *blocks)


def place_along_y(place, *blocks):
    place_messages(place[6] == 1, *blocks)


def take_along_x(place, *blocks):
    take_messages(place[4] == 1, place[5] == 1, place[0] == 1, *blocks)


def take_along_y(place, *blocks):
    take_messages(place[6] == 1, place[1] == 1, place[2] == 1, *blocks)


def pack_first(u_in, material_in, intact_in, near, far, u, material_copy, ones, twos, threes, up, down, done):
    place = position()
    parts = [
        pltpu.make_async_copy(u_in, u, done.at[0]),
        pltpu.make_async_copy(material_in, material_copy, done.at[1]),
    ]
    for a, block in ((1, ones), (2, twos), (3, threes)):
        first = min(k for k in X_FLAG if OFFSETS[k][0] == a)
        source = intact_in.at[pl.ds(first, block.shape[0]), pl.ds(64 - 8 * a, 8 * a), :]
        parts.append(pltpu.make_async_copy(source, block, done.at[1 + a]))
    for part in parts:
        part.start()
    for part in parts:
        part.wait()
    for n in range(3):
        up[24 * n : 24 * n + 24, :] = u[64 * n + 40 : 64 * n + 64, :]
        down[24 * n : 24 * n + 24, :] = u[64 * n : 64 * n + 24, :]
    up[72:96, :] = material_copy[40:64, :].astype(F32)
    down[72:96, :] = material_copy[0:24, :].astype(F32)
    at = 96
    for block in (ones, twos, threes):
        size = block.shape[0] * block.shape[1]
        up[at : at + size, :] = block[...].astype(F32).reshape(size, 128)
        at += size
    place_along_x(place, up, down, near, far)


def widen(target, base, own, own_base, below, above, at):
    for x in range(-3, 11):
        if x < 0:
            tile = below[at + 8 * (x + 3) : at + 8 * (x + 3) + 8, :]
        elif x < 8:
            tile = own[own_base + 8 * x : own_base + 8 * x + 8, :]
        else:
            tile = above[at + 8 * (x - 8) : at + 8 * (x - 8) + 8, :]
        target[pl.ds(base + x + 3, 8, stride=16), :] = tile
    for x in (14, 15):
        target[pl.ds(base + x, 8, stride=16), :] = jnp.zeros((8, 128), F32)


def shifted_row(field, fields, c, column):
    return ((c + 3) * fields + field) * 224 + (column + 3) * 16


def store_shifts(target, field, fields, column, half, tile, along_z):
    for c in range(-3, 4):
        value = roll(tile, -c)
        if along_z and c:
            value = value + float(c)
        target[rows(shifted_row(field, fields, c, column) + 8 * half), :] = value


def pair_geometry(shifts, fields, column, a, c, own_x, own_y, own_z):
    at = 3 + a
    x = shifts[rows(shifted_row(0, fields, c, column) + at), :] - own_x
    y = shifts[rows(shifted_row(1, fields, c, column) + at), :] - own_y
    z = shifts[rows(shifted_row(2, fields, c, column) + at), :] - own_z
    return x, y, z, x * x + y * y + z * z


def band_sum(flags, incoming, shifts, sums):
    def column_sum(y, carry):
        own = [shifts[rows(shifted_row(n, 3, 0, y) + 3), :] for n in range(3)]
        total = jnp.zeros((8, 128), F32)
        own_x = {a: own[0] - float(a) for a in range(-3, 4)}
        for b in range(-3, 4):
            own_y = own[1] - float(b)
            part = None
            for a, c in directed(b):
                _, _, _, square = pair_geometry(shifts, 3, y + b, a, c, own_x[a], own_y, own[2])
                length = square * lax.rsqrt(square)
                stretch = length - math.sqrt(float(a * a + b * b + c * c))
                if (a, b, c) > (0, 0, 0):
                    flag = flags[rows(FLAG_BASE[INDEX[a, b, c]] + y * (8 + a) + a), :]
                else:
                    flag = incoming[rows((INDEX[-a, -b, -c] * 14 + y + b + 3) * 8), :]
                part = flag * stretch if part is None else part + flag * stretch
            if b:
                inside = jnp.logical_and(y + b >= 0, y + b < 8)
                part = jnp.where(inside, part, 0.0)
            total = total + part
        sums[rows(8 * y), :] = total
        return carry

    lax.fori_loop(0, 8, column_sum, 0)


def own_shifts(wide, shifts):
    def column(y, carry):
        for n in range(3):
            for half in range(2):
                tile = wide[rows(128 * n + 16 * y + 8 * half), :]
                store_shifts(shifts, n, 3, y, half, tile, n == 2)
        return carry

    lax.fori_loop(0, 8, column, 0)


def pack_y(wide, sums, up, down):
    for n in range(3):
        up[48 * n : 48 * n + 48, :] = wide[128 * n + 80 : 128 * n + 128, :]
        down[48 * n : 48 * n + 48, :] = wide[128 * n : 128 * n + 48, :]
    up[Y_SUM : Y_SUM + 24, :] = sums[40:64, :]
    down[Y_SUM : Y_SUM + 24, :] = sums[0:24, :]


def validity(place, b, c):
    lane = lax.broadcasted_iota(jnp.int32, (8, 128), 1)
    column = lax.broadcasted_iota(jnp.int32, (8, 128), 0)
    first_column = jnp.where(place[1] == 1, 0, -8)
    last_column = jnp.where(place[2] == 1, 8, 16)
    in_y = jnp.logical_and(column + b >= first_column, column + b < last_column)
    inside = jnp.logical_and(in_y, jnp.logical_and(lane + c >= 0, lane + c < 128))
    return jnp.where(inside, 1.0, 0.0).astype(F32)


def prepare_flags(
    u_in, material_in, intact, flags, incoming, u, material, near, far, up, down
):
    u[...] = u_in[...]
    material[...] = material_in[...].astype(F32)
    place = position()
    zero = place[3]
    last_x = jnp.where(place[0] == 1, 0.0, 1.0)
    for b in range(-3, 4):
        for c in range(-3, 4):
            valid = validity(place, b, c)
            leaving = valid * last_x
            for a in range(4):
                k = INDEX.get((a, b, c))
                if k is None:
                    continue
                for x in range(8):
                    tile = intact[64 * k + 8 * x : 64 * k + 8 * x + 8, :].astype(F32)
                    tile = tile * (leaving if x + a >= 8 else valid)
                    flags[pl.ds(FLAG_BASE[k] + a + x, 8, stride=8 + a), :] = tile

    def turn(y, carry):
        for k, (a, b, c) in enumerate(OFFSETS):
            tile = flags[rows(FLAG_BASE[k] + y * (8 + a)), :]
            incoming[rows((k * 14 + y + 3) * 8), :] = roll(tile, c)
        return carry

    lax.fori_loop(0, 8, turn, 0)
    for k, at in EARLY.items():
        a, b, c = OFFSETS[k]
        for n in range(abs(b)):
            column = 8 - b + n if b > 0 else n
            tile = flags[rows(zero + FLAG_BASE[k] + column * (8 + a) + a), :]
            (up if b > 0 else down)[at + 8 * n : at + 8 * n + 8, :] = tile
    place_along_y(place, up, down, near, far)


def band_first(
    u, material, near, far, own_flags, own_incoming,
    wide, wide_material, sums, near_y, far_y, flags, incoming, shifts, below, above, up, down,
):
    place = position()
    zero = place[3]
    take_along_x(place, near, far, below, above)
    for k, base in X_FLAG.items():
        a, b, c = OFFSETS[k]
        valid = validity(place, b, c)
        for t in range(a):
            tile = below[base + 8 * t : base + 8 * t + 8, :] * valid
            flags[pl.ds(FLAG_BASE[k] + t, 8, stride=8 + a), :] = tile
            incoming[pl.ds((k * 14 + 3) * 8 + t, 8, stride=8), :] = roll(tile, c)
    for n in range(3):
        widen(wide, 128 * n, u, 64 * n, below, above, 24 * n)
    widen(wide_material, 0, material, 0, below, above, 72)
    own_shifts(wide, shifts)
    band_sum(flags, incoming, shifts, sums)
    pack_y(wide, sums, up, down)
    up[Y_MATERIAL : Y_MATERIAL + 48, :] = wide_material[80:128, :]
    down[Y_MATERIAL : Y_MATERIAL + 48, :] = wide_material[0:48, :]
    for k, at in CORNER.items():
        a, b, c = OFFSETS[k]
        for n in range(abs(b) if a else 0):
            column = 8 - b + n if b > 0 else n
            copy_rows(up if b > 0 else down, zero + at + a * n, flags, zero + FLAG_BASE[k] + column * (8 + a), a)
    place_along_y(place, up, down, near_y, far_y)


def band_next(
    u, near, far, flags, incoming, wide, sums, near_y, far_y, shifts, below, above, up, down
):
    place = position()
    take_along_x(place, near, far, below, above)
    for n in range(3):
        widen(wide, 128 * n, u, 64 * n, below, above, 24 * n)
    own_shifts(wide, shifts)
    band_sum(flags, incoming, shifts, sums)
    pack_y(wide, sums, up, down)
    place_along_y(place, up, down, near_y, far_y)


def wide_tile(wide, before, after, field, column, half):
    if column < 0:
        return before[rows(48 * field + 16 * (column + 3) + 8 * half), :]
    if column < 8:
        return wide[rows(128 * field + 16 * column + 8 * half), :]
    return after[rows(48 * field + 16 * (column - 8) + 8 * half), :]


def strip_theta(first, wide, flags, incoming, sums, near, far, *rest):
    place = position()
    if not first:
        before_flags, after_flags, *rest = rest
    else:
        early_near, early_far, *rest = rest
    theta, near_x, far_x, before, after, *rest = rest
    zero = place[3]
    if first:
        all_incoming, shifts, up, down, early_before, early_after, late_before, late_after = rest
        take_along_y(place, early_near, early_far, early_before, early_after)
        take_along_y(place, near, far, late_before, late_after)
        before_flags, after_flags = before, after
        before[0:Y_FLAGS, :] = late_before[0:Y_FLAGS, :]
        after[0:Y_FLAGS, :] = late_after[0:Y_FLAGS, :]
        for k, at in EARLY.items():
            a, b, c = OFFSETS[k]
            target, to = (before, Y_UP_FLAG[k]) if b > 0 else (after, Y_DOWN_FLAG[k])
            early, late = (early_before, late_before) if b > 0 else (early_after, late_after)
            for n in range(abs(b)):
                block = zero + to + n * (8 + a)
                if a:
                    copy_rows(target, block, late, zero + CORNER[k] + a * n, a)
                copy_rows(target, block + a, early, at + 8 * n, 8)
        own_incoming, incoming = incoming, all_incoming

        def keep(k, carry):
            copy_rows(incoming, (k * 14 + 3) * 8, own_incoming, (k * 14 + 3) * 8, 64)
            return carry

        lax.fori_loop(0, len(OFFSETS), keep, 0)
        for k, (a, b, c) in enumerate(OFFSETS):
            for n in range(abs(b)):
                if b > 0:
                    tile = before_flags[rows(zero + Y_UP_FLAG[k] + n * (8 + a)), :]
                    incoming[rows((k * 14 + 3 - b + n) * 8), :] = roll(tile, c)
                else:
                    tile = after_flags[rows(zero + Y_DOWN_FLAG[k] + n * (8 + a)), :]
                    incoming[rows((k * 14 + 11 + n) * 8), :] = roll(tile, c)
    else:
        take_along_y(place, near, far, before, after)
        shifts, up, down = rest
    for column in (-3, -2, -1, 0, 1, 2, 5, 6, 7, 8, 9, 10):
        for n in range(3):
            for half in range(2):
                tile = wide_tile(wide, before, after, n, column, half)
                store_shifts(shifts, n, 3, column, half, tile, n == 2)
    for block in (up, down):
        block[40:48, :] = jnp.zeros((8, 128), F32)
    for column in range(-3, 11):
        if column < 0:
            total = before[rows(Y_SUM + 8 * (column + 3)), :]
            partners = range(-column, 4)
        elif column < 8:
            total = sums[rows(8 * column), :]
            partners = [b for b in range(-3, 4) if not 0 <= column + b < 8]
        else:
            total = after[rows(Y_SUM + 8 * (column - 8)), :]
            partners = range(-3, 8 - column)
        own = [shifts[rows(zero + shifted_row(n, 3, 0, column) + 3), :] for n in range(3)] if len(partners) else None
        for b in partners:
            own_y = own[1] - float(b)
            for a, c in directed(b):
                own_x = own[0] - float(a)
                _, _, _, square = pair_geometry(shifts, 3, zero * 0 + column + b, a, c, own_x, own_y, own[2])
                length = square * lax.rsqrt(square)
                stretch = length - math.sqrt(float(a * a + b * b + c * c))
                if (a, b, c) > (0, 0, 0):
                    k = INDEX[a, b, c]
                    if column < 0:
                        flag = before_flags[rows(zero + Y_UP_FLAG[k] + (column + b) * (8 + a) + a), :]
                    elif column < 8:
                        flag = flags[rows(zero + FLAG_BASE[k] + column * (8 + a) + a), :]
                    else:
                        flag = after_flags[rows(zero + Y_DOWN_FLAG[k] + (column - 8) * (8 + a) + a), :]
                else:
                    flag = incoming[rows((INDEX[-a, -b, -c] * 14 + column + b + 3) * 8), :]
                total = total + flag * stretch
        theta[rows(8 * (column + 3)), :] = total
        up[rows(zero + 3 * (column + 3), 3), :] = theta[rows(zero + 8 * (column + 3) + 5, 3), :]
        down[rows(zero + 3 * (column + 3), 3), :] = theta[rows(zero + 8 * (column + 3), 3), :]
    place_along_x(place, up, down, near_x, far_x)


def pick(numbers, values):
    result = jnp.broadcast_to(values[CLASSES - 1 : CLASSES, :], numbers.shape)
    for n in range(CLASSES - 1):
        result = jnp.where(numbers == float(n), values[n : n + 1, :], result)
    return result


def advance(last, table, u, v, wide, before, after, wide_material, before_material, after_material,
            theta, near, far, flags, incoming, *rest):
    if last:
        new_u, new_v, force, shifts, wide_theta, below, above = rest
    else:
        new_u, new_v, near_x, far_x, shifts, wide_theta, below, above, up, down = rest
        force = None
    place = position()
    zero = place[3]
    take_along_x(place, near, far, below, above)
    bulk, shear, inertia = table[0:8, :], table[8:16, :], table[16:24, :]
    twist = shear * (15.0 / VOLUME)
    press = (bulk * 3.0 - shear * 5.0) * (3.0 / (VOLUME * VOLUME))
    for column in range(-3, 11):
        at = 16 * (column + 3)
        wide_theta[rows(zero + at + 3), :] = theta[8 * (column + 3) : 8 * (column + 3) + 8, :]
        wide_theta[rows(zero + at, 3), :] = below[rows(zero + 3 * (column + 3), 3), :]
        wide_theta[rows(zero + at + 11, 3), :] = above[rows(zero + 3 * (column + 3), 3), :]
        wide_theta[rows(zero + at + 14, 2), :] = jnp.zeros((2, 128), F32)
        for half in range(2):
            for n in range(3):
                tile = wide_tile(wide, before, after, n, column, half)
                store_shifts(shifts, n, 5, column, half, tile, n == 2)
            if column < 0:
                number = before_material[rows(Y_MATERIAL + 16 * (column + 3) + 8 * half), :]
            elif column < 8:
                number = wide_material[rows(16 * column + 8 * half), :]
            else:
                number = after_material[rows(Y_MATERIAL + 16 * (column - 8) + 8 * half), :]
            twisting = pick(number, twist)
            pressing = pick(number, press) * wide_theta[rows(at + 8 * half), :] - twisting
            store_shifts(shifts, 3, 5, column, half, pressing, False)
            store_shifts(shifts, 4, 5, column, half, twisting, False)

    def column_force(y, carry):
        own = [shifts[rows(shifted_row(n, 5, 0, y) + 3), :] for n in range(5)]
        own_x = {a: own[0] - float(a) for a in range(-3, 4)}
        total = [jnp.zeros((8, 128), F32) for _ in range(3)]
        for b in range(-3, 4):
            own_y = own[1] - float(b)
            for a, c in directed(b):
                *vector, square = pair_geometry(shifts, 5, y + b, a, c, own_x[a], own_y, own[2])
                inverse = lax.rsqrt(square)
                pressing = shifts[rows(shifted_row(3, 5, c, y + b) + 3 + a), :] + own[3]
                twisting = shifts[rows(shifted_row(4, 5, c, y + b) + 3 + a), :] + own[4]
                if (a, b, c) > (0, 0, 0):
                    flag = flags[rows(FLAG_BASE[INDEX[a, b, c]] + y * (8 + a) + a), :]
                else:
                    flag = incoming[rows((INDEX[-a, -b, -c] * 14 + y + b + 3) * 8), :]
                size = flag * (pressing * inverse + twisting * (1.0 / math.sqrt(float(a * a + b * b + c * c))))
                total = [t + size * w for t, w in zip(total, vector)]
        number = wide_material[rows(16 * y + 3), :]
        mass = pick(number, inertia)
        for n in range(3):
            at = pl.ds(64 * n + y, 8, stride=8)
            speed = v[at, :] + TIME_STEP * total[n] / mass
            new_v[at, :] = speed
            new_u[at, :] = u[at, :] + TIME_STEP * speed
            if last:
                force[at, :] = total[n]
        return carry

    lax.fori_loop(0, 8, column_force, 0)
    if not last:
        for n in range(3):
            up[24 * n : 24 * n + 24, :] = new_u[64 * n + 40 : 64 * n + 64, :]
            down[24 * n : 24 * n + 24, :] = new_u[64 * n : 64 * n + 24, :]
        place_along_x(place, up, down, near_x, far_x)


VMEM = pl.BlockSpec(memory_space=pltpu.VMEM)
IN_HBM = pl.BlockSpec(memory_space=pltpu.HBM)


def call(body, outputs, scratch, *arguments, flops=0, aliases={}, place=VMEM, limit=24):
    shapes = [jax.ShapeDtypeStruct((n, 128), F32) for n in outputs]
    traffic = 512 * sum(outputs) + sum(4 * x.size for x in arguments)
    return pl.pallas_call(
        body,
        out_shape=shapes,
        in_specs=[place] * len(arguments),
        out_specs=[VMEM] * len(shapes),
        scratch_shapes=[pltpu.VMEM((n, 128), F32) if isinstance(n, int) else n for n in scratch],
        input_output_aliases=aliases,
        compiler_params=pltpu.CompilerParams(vmem_limit_bytes=limit << 20),
        cost_estimate=pl.CostEstimate(flops=flops, bytes_accessed=traffic, transcendentals=0),
    )(*arguments)


def swap_pairs(far, near, axis):
    sizes = {name: lax.axis_size(name) for name in ("gx", "gy")}
    other = "gy" if axis == "gx" else "gx"
    size = sizes[axis]

    def device(along, across):
        at = {axis: along, other: across}
        return at["gx"] * sizes["gy"] + at["gy"]

    swaps = []
    for start in (0, 1):
        pairs = []
        for across in range(sizes[other]):
            for along in range(size):
                partner = along + 1 if (along - start) % 2 == 0 else along - 1
                inside = 0 <= partner < size
                target = device(partner, across) if inside else device(along, across ^ 1)
                pairs.append((device(along, across), target))
        swaps.append(pairs)
    far = lax.ppermute(far, ("gx", "gy"), swaps[1])
    near = lax.ppermute(near, ("gx", "gy"), swaps[0])
    return far, near


def on_device(displacement, velocity, intact, material, bulk_modulus, shear_modulus, density):
    shape = displacement.shape
    bonds = len(OFFSETS)
    u, v = displacement.reshape(192, 128), velocity.reshape(192, 128)
    material = material.reshape(64, 128)
    table = jnp.broadcast_to(jnp.concatenate([bulk_modulus, shear_modulus, density])[:, None], (3 * CLASSES, 128))
    all_rows = bonds * 14 * 8
    counts = [sum(offset[0] == a for offset in OFFSETS) for a in (1, 2, 3)]
    blocks = [pltpu.VMEM((count, 8 * a, 128), jnp.int32) for a, count in zip((1, 2, 3), counts)]
    far, near = call(
        pack_first, [X_UP_ROWS, X_UP_ROWS],
        [
            pltpu.VMEM((192, 128), F32), pltpu.VMEM((64, 128), jnp.int32), *blocks, X_UP_ROWS, X_UP_ROWS,
            pltpu.SemaphoreType.DMA((5,)),
        ],
        u, material, intact.reshape(bonds, 64, 128), place=IN_HBM, limit=59,
    )
    flags, incoming, u, material, early_far, early_near = call(
        prepare_flags, [FLAG_ROWS, all_rows, 192, 64, EARLY_ROWS, EARLY_ROWS], [EARLY_ROWS, EARLY_ROWS],
        u, material, intact.reshape(bonds * 64, 128), flops=bonds * 8192 * 4,
    )
    far, near = swap_pairs(far, near, "gx")
    early_far, early_near = swap_pairs(early_far, early_near, "gy")
    wide, wide_material, sums, far, near, flags, incoming = call(
        band_first,
        [384, 128, 64, CORNER_ROWS, CORNER_ROWS, FLAG_ROWS, all_rows],
        [7 * 3 * 224, X_UP_ROWS, X_DOWN_ROWS, CORNER_ROWS, CORNER_ROWS],
        u, material, far, near, flags, incoming, aliases={4: 5, 5: 6},
    )
    far, near = swap_pairs(far, near, "gy")
    for step in range(STEPS):
        if step:
            far, near = swap_pairs(far, near, "gx")
            wide, sums, far, near = call(
                band_next, [384, 64, Y_MATERIAL, Y_MATERIAL], [7 * 3 * 224, 72, 72, Y_MATERIAL, Y_MATERIAL],
                u, far, near, flags, incoming,
            )
            far, near = swap_pairs(far, near, "gy")
            theta, far, near, before, after = call(
                functools.partial(strip_theta, False), [112, 48, 48, Y_MATERIAL, Y_MATERIAL], [7 * 3 * 224, 48, 48],
                wide, flags, incoming, sums, far, near, first_before, first_after,
            )
        else:
            theta, far, near, before, after, incoming = call(
                functools.partial(strip_theta, True), [112, 48, 48, Y_ROWS, Y_ROWS, all_rows],
                [7 * 3 * 224, 48, 48, EARLY_ROWS, EARLY_ROWS, CORNER_ROWS, CORNER_ROWS],
                wide, flags, incoming, sums, far, near, early_far, early_near,
            )
            first_before, first_after = before, after
        far, near = swap_pairs(far, near, "gx")
        last = step == STEPS - 1
        u, v, *more = call(
            functools.partial(advance, last), [192, 192] + ([192] if last else [72, 72]),
            [7 * 5 * 224, 224, 48, 48] + ([] if last else [72, 72]),
            table, u, v, wide, before, after, wide_material, first_before, first_after,
            theta, far, near, flags, incoming,
        )
        if last:
            force = more[0]
        else:
            far, near = more
    return u.reshape(shape), v.reshape(shape), force.reshape(shape)


def solution(mesh):
    return jax.shard_map(
        on_device,
        mesh=mesh,
        in_specs=(
            P(None, "gx", "gy", None),
            P(None, "gx", "gy", None),
            P(None, "gx", "gy", None),
            P("gx", "gy", None),
            P(),
            P(),
            P(),
        ),
        out_specs=(P(None, "gx", "gy", None), P(None, "gx", "gy", None), P(None, "gx", "gy", None)),
        check_vma=False,
    )
```

```python
import functools
import math

import jax
import jax.numpy as jnp
from jax import lax
from jax.experimental import pallas as pl
from jax.experimental.pallas import tpu as pltpu
from jax.sharding import PartitionSpec as P

STEPS = 2
TIME_STEP = 0.02
F32 = jnp.float32
CLASSES = 8

OFFSETS = [
    (a, b, c)
    for a in range(-3, 4)
    for b in range(-3, 4)
    for c in range(-3, 4)
    if a * a + b * b + c * c <= 9 and (a, b, c) > (0, 0, 0)
]
INDEX = {offset: k for k, offset in enumerate(OFFSETS)}
VOLUME = 2.0 * sum(math.sqrt(float(a * a + b * b + c * c)) for a, b, c in OFFSETS)


def directed(b):
    return [
        (a, c)
        for a in range(-3, 4)
        for c in range(-3, 4)
        if 0 < a * a + b * b + c * c <= 9
    ]


FLAG_BASE, _row = [], 0
for _a, _b, _c in OFFSETS:
    FLAG_BASE.append(_row)
    _row += 8 * (8 + _a)
FLAG_ROWS = _row

X_FLAG, _row = {}, 96
for _k, (_a, _b, _c) in enumerate(OFFSETS):
    if _a:
        X_FLAG[_k] = _row
        _row += 8 * _a
X_UP_ROWS, X_DOWN_ROWS = _row, 96

Y_SUM, Y_MATERIAL, Y_FLAGS = 144, 168, 216
Y_UP_FLAG, Y_DOWN_FLAG, _up, _down = {}, {}, Y_FLAGS, Y_FLAGS
for _k, (_a, _b, _c) in enumerate(OFFSETS):
    if _b > 0:
        Y_UP_FLAG[_k] = _up
        _up += _b * (8 + _a)
    elif _b < 0:
        Y_DOWN_FLAG[_k] = _down
        _down += -_b * (8 + _a)
Y_ROWS = -(-max(_up, _down) // 8) * 8

EARLY, CORNER = {}, {}
for _sign in (1, -1):
    _early, _corner = 0, Y_FLAGS
    for _k, (_a, _b, _c) in enumerate(OFFSETS):
        if _b * _sign > 0:
            EARLY[_k], CORNER[_k] = _early, _corner
            _early += abs(_b) * 8
            _corner += abs(_b) * _a
EARLY_ROWS = max(EARLY[k] + 8 * abs(OFFSETS[k][1]) for k in EARLY)
CORNER_ROWS = -(-max(CORNER[k] + abs(OFFSETS[k][1]) * OFFSETS[k][0] for k in CORNER) // 8) * 8


def rows(start, count=8):
    return pl.ds(start, count)


def copy_rows(target, to, source, at, count):
    done = 0
    while done < count:
        size = min(8, count - done)
        target[rows(to + done, size), :] = source[rows(at + done, size), :]
        done += size


def roll(value, shift):
    return value if shift % 128 == 0 else pltpu.roll(value, shift % 128, 1)


def position():
    gx, gy = lax.axis_index("gx"), lax.axis_index("gy")
    last_x, last_y = lax.axis_size("gx") - 1, lax.axis_size("gy") - 1
    flags = [gx == last_x, gy == 0, gy == last_y, gy < 0, gx % 2 == 0, gx == 0, gy % 2 == 0]
    return [jnp.where(flag, 1, 0) for flag in flags]


def place_messages(even, up, down, far, near):
    near[...] = jnp.where(even, up[...], down[...])
    far[...] = jnp.where(even, down[...], up[...])


def take_messages(even, first, last, far, near, below, above):
    size = above.shape[0]
    below[...] = jnp.where(first, 0.0, jnp.where(even, far[...], near[...]))
    above[...] = jnp.where(last, 0.0, jnp.where(even, near[0:size, :], far[0:size, :]))


def place_along_x(place, *blocks):
    place_messages(place[4] == 1, *blocks)


def place_along_y(place, *blocks):
    place_messages(place[6] == 1, *blocks)


def take_along_x(place, *blocks):
    take_messages(place[4] == 1, place[5] == 1, place[0] == 1, *blocks)


def take_along_y(place, *blocks):
    take_messages(place[6] == 1, place[1] == 1, place[2] == 1, *blocks)


def pack_first(u_in, material_in, intact_in, near, far, u, material_copy, ones, twos, threes, up, down, done):
    place = position()
    parts = [
        pltpu.make_async_copy(u_in, u, done.at[0]),
        pltpu.make_async_copy(material_in, material_copy, done.at[1]),
    ]
    for a, block in ((1, ones), (2, twos), (3, threes)):
        first = min(k for k in X_FLAG if OFFSETS[k][0] == a)
        source = intact_in.at[pl.ds(first, block.shape[0]), pl.ds(64 - 8 * a, 8 * a), :]
        parts.append(pltpu.make_async_copy(source, block, done.at[1 + a]))
    for part in parts:
        part.start()
    for part in parts:
        part.wait()
    for n in range(3):
        up[24 * n : 24 * n + 24, :] = u[64 * n + 40 : 64 * n + 64, :]
        down[24 * n : 24 * n + 24, :] = u[64 * n : 64 * n + 24, :]
    up[72:96, :] = material_copy[40:64, :].astype(F32)
    down[72:96, :] = material_copy[0:24, :].astype(F32)
    at = 96
    for block in (ones, twos, threes):
        size = block.shape[0] * block.shape[1]
        up[at : at + size, :] = block[...].astype(F32).reshape(size, 128)
        at += size
    place_along_x(place, up, down, near, far)


def widen(target, base, own, own_base, below, above, at):
    for x in range(-3, 11):
        if x < 0:
            tile = below[at + 8 * (x + 3) : at + 8 * (x + 3) + 8, :]
        elif x < 8:
            tile = own[own_base + 8 * x : own_base + 8 * x + 8, :]
        else:
            tile = above[at + 8 * (x - 8) : at + 8 * (x - 8) + 8, :]
        target[pl.ds(base + x + 3, 8, stride=16), :] = tile
    for x in (14, 15):
        target[pl.ds(base + x, 8, stride=16), :] = jnp.zeros((8, 128), F32)


def shifted_row(field, fields, c, column):
    return ((c + 3) * fields + field) * 224 + (column + 3) * 16


def store_shifts(target, field, fields, column, half, tile, along_z):
    for c in range(-3, 4):
        value = roll(tile, -c)
        if along_z and c:
            value = value + float(c)
        target[rows(shifted_row(field, fields, c, column) + 8 * half), :] = value


def pair_geometry(shifts, fields, column, a, c, own_x, own_y, own_z):
    at = 3 + a
    x = shifts[rows(shifted_row(0, fields, c, column) + at), :] - own_x
    y = shifts[rows(shifted_row(1, fields, c, column) + at), :] - own_y
    z = shifts[rows(shifted_row(2, fields, c, column) + at), :] - own_z
    return x, y, z, x * x + y * y + z * z


def band_sum(flags, incoming, shifts, sums):
    def column_sum(y, carry):
        own = [shifts[rows(shifted_row(n, 3, 0, y) + 3), :] for n in range(3)]
        total = jnp.zeros((8, 128), F32)
        own_x = {a: own[0] - float(a) for a in range(-3, 4)}
        for b in range(-3, 4):
            own_y = own[1] - float(b)
            part = None
            for a, c in directed(b):
                _, _, _, square = pair_geometry(shifts, 3, y + b, a, c, own_x[a], own_y, own[2])
                length = square * lax.rsqrt(square)
                stretch = length - math.sqrt(float(a * a + b * b + c * c))
                if (a, b, c) > (0, 0, 0):
                    flag = flags[rows(FLAG_BASE[INDEX[a, b, c]] + y * (8 + a) + a), :]
                else:
                    flag = incoming[rows((INDEX[-a, -b, -c] * 14 + y + b + 3) * 8), :]
                part = flag * stretch if part is None else part + flag * stretch
            if b:
                inside = jnp.logical_and(y + b >= 0, y + b < 8)
                part = jnp.where(inside, part, 0.0)
            total = total + part
        sums[rows(8 * y), :] = total
        return carry

    lax.fori_loop(0, 8, column_sum, 0)


def own_shifts(wide, shifts):
    def column(y, carry):
        for n in range(3):
            for half in range(2):
                tile = wide[rows(128 * n + 16 * y + 8 * half), :]
                store_shifts(shifts, n, 3, y, half, tile, n == 2)
        return carry

    lax.fori_loop(0, 8, column, 0)


def pack_y(wide, sums, up, down):
    for n in range(3):
        up[48 * n : 48 * n + 48, :] = wide[128 * n + 80 : 128 * n + 128, :]
        down[48 * n : 48 * n + 48, :] = wide[128 * n : 128 * n + 48, :]
    up[Y_SUM : Y_SUM + 24, :] = sums[40:64, :]
    down[Y_SUM : Y_SUM + 24, :] = sums[0:24, :]


def validity(place, b, c):
    lane = lax.broadcasted_iota(jnp.int32, (8, 128), 1)
    column = lax.broadcasted_iota(jnp.int32, (8, 128), 0)
    first_column = jnp.where(place[1] == 1, 0, -8)
    last_column = jnp.where(place[2] == 1, 8, 16)
    in_y = jnp.logical_and(column + b >= first_column, column + b < last_column)
    inside = jnp.logical_and(in_y, jnp.logical_and(lane + c >= 0, lane + c < 128))
    return jnp.where(inside, 1.0, 0.0).astype(F32)


def prepare_flags(
    u_in, material_in, intact, flags, incoming, u, material, near, far, up, down
):
    u[...] = u_in[...]
    material[...] = material_in[...].astype(F32)
    place = position()
    zero = place[3]
    last_x = jnp.where(place[0] == 1, 0.0, 1.0)
    for b in range(-3, 4):
        for c in range(-3, 4):
            valid = validity(place, b, c)
            leaving = valid * last_x
            for a in range(4):
                k = INDEX.get((a, b, c))
                if k is None:
                    continue
                for x in range(8):
                    tile = intact[64 * k + 8 * x : 64 * k + 8 * x + 8, :].astype(F32)
                    tile = tile * (leaving if x + a >= 8 else valid)
                    flags[pl.ds(FLAG_BASE[k] + a + x, 8, stride=8 + a), :] = tile

    def turn(y, carry):
        for k, (a, b, c) in enumerate(OFFSETS):
            tile = flags[rows(FLAG_BASE[k] + y * (8 + a)), :]
            incoming[rows((k * 14 + y + 3) * 8), :] = roll(tile, c)
        return carry

    lax.fori_loop(0, 8, turn, 0)
    for k, at in EARLY.items():
        a, b, c = OFFSETS[k]
        for n in range(abs(b)):
            column = 8 - b + n if b > 0 else n
            tile = flags[rows(zero + FLAG_BASE[k] + column * (8 + a) + a), :]
            (up if b > 0 else down)[at + 8 * n : at + 8 * n + 8, :] = tile
    place_along_y(place, up, down, near, far)


def band_first(
    u, material, near, far, own_flags, own_incoming,
    wide, wide_material, sums, near_y, far_y, flags, incoming, shifts, below, above, up, down,
):
    place = position()
    zero = place[3]
    take_along_x(place, near, far, below, above)
    for k, base in X_FLAG.items():
        a, b, c = OFFSETS[k]
        valid = validity(place, b, c)
        for t in range(a):
            tile = below[base + 8 * t : base + 8 * t + 8, :] * valid
            flags[pl.ds(FLAG_BASE[k] + t, 8, stride=8 + a), :] = tile
            incoming[pl.ds((k * 14 + 3) * 8 + t, 8, stride=8), :] = roll(tile, c)
    for n in range(3):
        widen(wide, 128 * n, u, 64 * n, below, above, 24 * n)
    widen(wide_material, 0, material, 0, below, above, 72)
    own_shifts(wide, shifts)
    band_sum(flags, incoming, shifts, sums)
    pack_y(wide, sums, up, down)
    up[Y_MATERIAL : Y_MATERIAL + 48, :] = wide_material[80:128, :]
    down[Y_MATERIAL : Y_MATERIAL + 48, :] = wide_material[0:48, :]
    for k, at in CORNER.items():
        a, b, c = OFFSETS[k]
        for n in range(abs(b) if a else 0):
            column = 8 - b + n if b > 0 else n
            copy_rows(up if b > 0 else down, zero + at + a * n, flags, zero + FLAG_BASE[k] + column * (8 + a), a)
    place_along_y(place, up, down, near_y, far_y)


def band_next(
    u, near, far, flags, incoming, wide, sums, near_y, far_y, shifts, below, above, up, down
):
    place = position()
    take_along_x(place, near, far, below, above)
    for n in range(3):
        widen(wide, 128 * n, u, 64 * n, below, above, 24 * n)
    own_shifts(wide, shifts)
    band_sum(flags, incoming, shifts, sums)
    pack_y(wide, sums, up, down)
    place_along_y(place, up, down, near_y, far_y)


def wide_tile(wide, before, after, field, column, half):
    if column < 0:
        return before[rows(48 * field + 16 * (column + 3) + 8 * half), :]
    if column < 8:
        return wide[rows(128 * field + 16 * column + 8 * half), :]
    return after[rows(48 * field + 16 * (column - 8) + 8 * half), :]


def strip_theta(first, wide, flags, incoming, sums, own_shifts, near, far, *rest):
    place = position()
    if not first:
        before_flags, after_flags, *rest = rest
    else:
        early_near, early_far, *rest = rest
    if first:
        theta, near_x, far_x, before, after, shifts, *rest = rest
    else:
        theta, near_x, far_x, shifts, before, after, *rest = rest
    zero = place[3]
    if first:
        all_incoming, up, down, early_before, early_after, late_before, late_after = rest
        take_along_y(place, early_near, early_far, early_before, early_after)
        take_along_y(place, near, far, late_before, late_after)
        before_flags, after_flags = before, after
        before[0:Y_FLAGS, :] = late_before[0:Y_FLAGS, :]
        after[0:Y_FLAGS, :] = late_after[0:Y_FLAGS, :]
        for k, at in EARLY.items():
            a, b, c = OFFSETS[k]
            target, to = (before, Y_UP_FLAG[k]) if b > 0 else (after, Y_DOWN_FLAG[k])
            early, late = (early_before, late_before) if b > 0 else (early_after, late_after)
            for n in range(abs(b)):
                block = zero + to + n * (8 + a)
                if a:
                    copy_rows(target, block, late, zero + CORNER[k] + a * n, a)
                copy_rows(target, block + a, early, at + 8 * n, 8)
        own_incoming, incoming = incoming, all_incoming

        def keep(k, carry):
            copy_rows(incoming, (k * 14 + 3) * 8, own_incoming, (k * 14 + 3) * 8, 64)
            return carry

        lax.fori_loop(0, len(OFFSETS), keep, 0)
        for k, (a, b, c) in enumerate(OFFSETS):
            for n in range(abs(b)):
                if b > 0:
                    tile = before_flags[rows(zero + Y_UP_FLAG[k] + n * (8 + a)), :]
                    incoming[rows((k * 14 + 3 - b + n) * 8), :] = roll(tile, c)
                else:
                    tile = after_flags[rows(zero + Y_DOWN_FLAG[k] + n * (8 + a)), :]
                    incoming[rows((k * 14 + 11 + n) * 8), :] = roll(tile, c)
    else:
        take_along_y(place, near, far, before, after)
        up, down = rest
    for column in (-3, -2, -1, 8, 9, 10):
        for n in range(3):
            for half in range(2):
                tile = wide_tile(wide, before, after, n, column, half)
                store_shifts(shifts, n, 3, column, half, tile, n == 2)
    for block in (up, down):
        block[40:48, :] = jnp.zeros((8, 128), F32)
    for column in range(-3, 11):
        if column < 0:
            total = before[rows(Y_SUM + 8 * (column + 3)), :]
            partners = range(-column, 4)
        elif column < 8:
            total = sums[rows(8 * column), :]
            partners = [b for b in range(-3, 4) if not 0 <= column + b < 8]
        else:
            total = after[rows(Y_SUM + 8 * (column - 8)), :]
            partners = range(-3, 8 - column)
        own = [shifts[rows(zero + shifted_row(n, 3, 0, column) + 3), :] for n in range(3)] if len(partners) else None
        for b in partners:
            own_y = own[1] - float(b)
            for a, c in directed(b):
                own_x = own[0] - float(a)
                _, _, _, square = pair_geometry(shifts, 3, zero * 0 + column + b, a, c, own_x, own_y, own[2])
                length = square * lax.rsqrt(square)
                stretch = length - math.sqrt(float(a * a + b * b + c * c))
                if (a, b, c) > (0, 0, 0):
                    k = INDEX[a, b, c]
                    if column < 0:
                        flag = before_flags[rows(zero + Y_UP_FLAG[k] + (column + b) * (8 + a) + a), :]
                    elif column < 8:
                        flag = flags[rows(zero + FLAG_BASE[k] + column * (8 + a) + a), :]
                    else:
                        flag = after_flags[rows(zero + Y_DOWN_FLAG[k] + (column - 8) * (8 + a) + a), :]
                else:
                    flag = incoming[rows((INDEX[-a, -b, -c] * 14 + column + b + 3) * 8), :]
                total = total + flag * stretch
        theta[rows(8 * (column + 3)), :] = total
        up[rows(zero + 3 * (column + 3), 3), :] = theta[rows(zero + 8 * (column + 3) + 5, 3), :]
        down[rows(zero + 3 * (column + 3), 3), :] = theta[rows(zero + 8 * (column + 3), 3), :]
    place_along_x(place, up, down, near_x, far_x)


def pick(numbers, values):
    result = jnp.broadcast_to(values[CLASSES - 1 : CLASSES, :], numbers.shape)
    for n in range(CLASSES - 1):
        result = jnp.where(numbers == float(n), values[n : n + 1, :], result)
    return result


def advance(last, table, u, v, shifts, wide_material, before_material, after_material,
            theta, near, far, flags, incoming, *rest):
    if last:
        new_u, new_v, force, loads, wide_theta, below, above = rest
    else:
        new_u, new_v, near_x, far_x, loads, wide_theta, below, above, up, down = rest
        force = None
    place = position()
    zero = place[3]
    take_along_x(place, near, far, below, above)
    bulk, shear, inertia = table[0:8, :], table[8:16, :], table[16:24, :]
    twist = shear * (15.0 / VOLUME)
    press = (bulk * 3.0 - shear * 5.0) * (3.0 / (VOLUME * VOLUME))
    for column in range(-3, 11):
        at = 16 * (column + 3)
        wide_theta[rows(zero + at + 3), :] = theta[8 * (column + 3) : 8 * (column + 3) + 8, :]
        wide_theta[rows(zero + at, 3), :] = below[rows(zero + 3 * (column + 3), 3), :]
        wide_theta[rows(zero + at + 11, 3), :] = above[rows(zero + 3 * (column + 3), 3), :]
        wide_theta[rows(zero + at + 14, 2), :] = jnp.zeros((2, 128), F32)
        for half in range(2):
            if column < 0:
                number = before_material[rows(Y_MATERIAL + 16 * (column + 3) + 8 * half), :]
            elif column < 8:
                number = wide_material[rows(16 * column + 8 * half), :]
            else:
                number = after_material[rows(Y_MATERIAL + 16 * (column - 8) + 8 * half), :]
            twisting = pick(number, twist)
            pressing = pick(number, press) * wide_theta[rows(at + 8 * half), :] - twisting
            store_shifts(loads, 0, 2, column, half, pressing, False)
            store_shifts(loads, 1, 2, column, half, twisting, False)

    def column_force(y, carry):
        own = [shifts[rows(shifted_row(n, 3, 0, y) + 3), :] for n in range(3)]
        own += [loads[rows(shifted_row(n, 2, 0, y) + 3), :] for n in range(2)]
        own_x = {a: own[0] - float(a) for a in range(-3, 4)}
        total = [jnp.zeros((8, 128), F32) for _ in range(3)]
        for b in range(-3, 4):
            own_y = own[1] - float(b)
            for a, c in directed(b):
                *vector, square = pair_geometry(shifts, 3, y + b, a, c, own_x[a], own_y, own[2])
                inverse = lax.rsqrt(square)
                pressing = loads[rows(shifted_row(0, 2, c, y + b) + 3 + a), :] + own[3]
                twisting = loads[rows(shifted_row(1, 2, c, y + b) + 3 + a), :] + own[4]
                if (a, b, c) > (0, 0, 0):
                    flag = flags[rows(FLAG_BASE[INDEX[a, b, c]] + y * (8 + a) + a), :]
                else:
                    flag = incoming[rows((INDEX[-a, -b, -c] * 14 + y + b + 3) * 8), :]
                size = flag * (pressing * inverse + twisting * (1.0 / math.sqrt(float(a * a + b * b + c * c))))
                total = [t + size * w for t, w in zip(total, vector)]
        number = wide_material[rows(16 * y + 3), :]
        mass = pick(number, inertia)
        for n in range(3):
            at = pl.ds(64 * n + y, 8, stride=8)
            speed = v[at, :] + TIME_STEP * total[n] / mass
            new_v[at, :] = speed
            new_u[at, :] = u[at, :] + TIME_STEP * speed
            if last:
                force[at, :] = total[n]
        return carry

    lax.fori_loop(0, 8, column_force, 0)
    if not last:
        for n in range(3):
            up[24 * n : 24 * n + 24, :] = new_u[64 * n + 40 : 64 * n + 64, :]
            down[24 * n : 24 * n + 24, :] = new_u[64 * n : 64 * n + 24, :]
        place_along_x(place, up, down, near_x, far_x)


VMEM = pl.BlockSpec(memory_space=pltpu.VMEM)
IN_HBM = pl.BlockSpec(memory_space=pltpu.HBM)


def call(body, outputs, scratch, *arguments, flops=0, aliases={}, place=VMEM, limit=24):
    shapes = [jax.ShapeDtypeStruct((n, 128), F32) for n in outputs]
    traffic = 512 * sum(outputs) + sum(4 * x.size for x in arguments)
    return pl.pallas_call(
        body,
        out_shape=shapes,
        in_specs=[place] * len(arguments),
        out_specs=[VMEM] * len(shapes),
        scratch_shapes=[pltpu.VMEM((n, 128), F32) if isinstance(n, int) else n for n in scratch],
        input_output_aliases=aliases,
        compiler_params=pltpu.CompilerParams(vmem_limit_bytes=limit << 20),
        cost_estimate=pl.CostEstimate(flops=flops, bytes_accessed=traffic, transcendentals=0),
    )(*arguments)


def swap_pairs(far, near, axis):
    sizes = {name: lax.axis_size(name) for name in ("gx", "gy")}
    other = "gy" if axis == "gx" else "gx"
    size = sizes[axis]

    def device(along, across):
        at = {axis: along, other: across}
        return at["gx"] * sizes["gy"] + at["gy"]

    swaps = []
    for start in (0, 1):
        pairs = []
        for across in range(sizes[other]):
            for along in range(size):
                partner = along + 1 if (along - start) % 2 == 0 else along - 1
                inside = 0 <= partner < size
                target = device(partner, across) if inside else device(along, across ^ 1)
                pairs.append((device(along, across), target))
        swaps.append(pairs)
    far = lax.ppermute(far, ("gx", "gy"), swaps[1])
    near = lax.ppermute(near, ("gx", "gy"), swaps[0])
    return far, near


def on_device(displacement, velocity, intact, material, bulk_modulus, shear_modulus, density):
    shape = displacement.shape
    bonds = len(OFFSETS)
    u, v = displacement.reshape(192, 128), velocity.reshape(192, 128)
    material = material.reshape(64, 128)
    table = jnp.broadcast_to(jnp.concatenate([bulk_modulus, shear_modulus, density])[:, None], (3 * CLASSES, 128))
    all_rows = bonds * 14 * 8
    counts = [sum(offset[0] == a for offset in OFFSETS) for a in (1, 2, 3)]
    blocks = [pltpu.VMEM((count, 8 * a, 128), jnp.int32) for a, count in zip((1, 2, 3), counts)]
    far, near = call(
        pack_first, [X_UP_ROWS, X_UP_ROWS],
        [
            pltpu.VMEM((192, 128), F32), pltpu.VMEM((64, 128), jnp.int32), *blocks, X_UP_ROWS, X_UP_ROWS,
            pltpu.SemaphoreType.DMA((5,)),
        ],
        u, material, intact.reshape(bonds, 64, 128), place=IN_HBM, limit=59,
    )
    flags, incoming, u, material, early_far, early_near = call(
        prepare_flags, [FLAG_ROWS, all_rows, 192, 64, EARLY_ROWS, EARLY_ROWS], [EARLY_ROWS, EARLY_ROWS],
        u, material, intact.reshape(bonds * 64, 128), flops=bonds * 8192 * 4,
    )
    far, near = swap_pairs(far, near, "gx")
    early_far, early_near = swap_pairs(early_far, early_near, "gy")
    wide, wide_material, sums, far, near, flags, incoming, shifts = call(
        band_first,
        [384, 128, 64, CORNER_ROWS, CORNER_ROWS, FLAG_ROWS, all_rows, 7 * 3 * 224],
        [X_UP_ROWS, X_DOWN_ROWS, CORNER_ROWS, CORNER_ROWS],
        u, material, far, near, flags, incoming, aliases={4: 5, 5: 6},
    )
    far, near = swap_pairs(far, near, "gy")
    for step in range(STEPS):
        if step:
            far, near = swap_pairs(far, near, "gx")
            wide, sums, far, near, shifts = call(
                band_next, [384, 64, Y_MATERIAL, Y_MATERIAL, 7 * 3 * 224], [72, 72, Y_MATERIAL, Y_MATERIAL],
                u, far, near, flags, incoming,
            )
            far, near = swap_pairs(far, near, "gy")
            theta, far, near, shifts = call(
                functools.partial(strip_theta, False), [112, 48, 48, 7 * 3 * 224],
                [Y_MATERIAL, Y_MATERIAL, 48, 48],
                wide, flags, incoming, sums, shifts, far, near, first_before, first_after,
                aliases={4: 3},
            )
        else:
            theta, far, near, before, after, shifts, incoming = call(
                functools.partial(strip_theta, True), [112, 48, 48, Y_ROWS, Y_ROWS, 7 * 3 * 224, all_rows],
                [48, 48, EARLY_ROWS, EARLY_ROWS, CORNER_ROWS, CORNER_ROWS],
                wide, flags, incoming, sums, shifts, far, near, early_far, early_near,
                aliases={4: 5},
            )
            first_before, first_after = before, after
        far, near = swap_pairs(far, near, "gx")
        last = step == STEPS - 1
        u, v, *more = call(
            functools.partial(advance, last), [192, 192] + ([192] if last else [72, 72]),
            [7 * 2 * 224, 224, 48, 48] + ([] if last else [72, 72]),
            table, u, v, shifts, wide_material, first_before, first_after,
            theta, far, near, flags, incoming,
        )
        if last:
            force = more[0]
        else:
            far, near = more
    return u.reshape(shape), v.reshape(shape), force.reshape(shape)


def solution(mesh):
    return jax.shard_map(
        on_device,
        mesh=mesh,
        in_specs=(
            P(None, "gx", "gy", None),
            P(None, "gx", "gy", None),
            P(None, "gx", "gy", None),
            P("gx", "gy", None),
            P(),
            P(),
            P(),
        ),
        out_specs=(P(None, "gx", "gy", None), P(None, "gx", "gy", None), P(None, "gx", "gy", None)),
        check_vma=False,
    )
```
